256 devices in a mesh: gx: 16 (over z_lo, y), gy: 4 (over x), gz: 4 (over z_hi, core).
Axes of the slice: x: 4, y: 4, z: 8 (z_hi: 2, z_lo: 4; z = z_hi * 4 + z_lo), core: 2. Of those that a mesh axis runs over, the one named last changes fastest.
Arguments:
- saved_thermal_values: float32 [256, 128, 1024], P('gx', 'gy', 'gz'), may hold values from -4 to 4
- saved_transformed_share: float32 [256, 128, 1024], P('gx', 'gy', 'gz'), may hold values from 0 to 0.9
- diffusion_numbers: float32 [256, 128, 1024], P('gx', 'gy', 'gz'), may hold values from 0.04 to 0.15
- transformation_status: int32 [256, 128, 1024], P('gx', 'gy', 'gz'), may hold values from 0 to 2
- boundary_conductances: float32 [1835008], P(('gx', 'gy', 'gz')), may hold values from 0.02 to 0.2
- boundary_voxel_locator: int32 [524288], P(('gx', 'gy', 'gz')), may hold values from 0 to 131071, as said below
- boundary_conductance_locator: int32 [524288], P(('gx', 'gy', 'gz')), may hold values from 0 to 1835007, as said below
- boundary_patch_extent: float32 [524288], P(('gx', 'gy', 'gz')), may hold values from 0.5 to 1.5
- boundary_active_entries: int32 [256], P(('gx', 'gy', 'gz')), may hold values from 1024 to 2048, as said below
- thermal_error_factor: float32 [256, 128, 1024], P('gx', 'gy', 'gz'), may hold values from -6 to 6
- product_error_factor: float32 [256, 128, 1024], P('gx', 'gy', 'gz'), may hold values from -6 to 6
Outputs:
- temp_final: float32 [256, 128, 1024], P('gx', 'gy', 'gz')
- phase_final: float32 [256, 128, 1024], P('gx', 'gy', 'gz')
- transfer_sensitivity: float32 [1835008], P(('gx', 'gy', 'gz'))
The draws below stay inside these ranges and needn't reach their ends.
Inputs may be any that keep to these rules, and one draw needn't show every extreme that they name: `boundary_voxel_locator`: within each brick's 2048 slots (aligned blocks of the array), the cell indices are distinct and increasing. `boundary_conductance_locator`: A slot of a brick whose gx index is i names a coefficient in [i * 114688, (i + 1) * 114688). `boundary_active_entries`: entry d is the number of live leading slots of brick d (flat over gx, gy, gz); the others are empty. Some brick has all 2048 slots live.
All inputs are finite; a program needn't handle non-finite values.
Results may differ from the reference program's by a relative error of at most 0.00002.
Values sent between devices are 32-bit elements; how exact they have to be, the bound alone decides.
A program may use at most 64 MiB of HBM per device.

```python
import math
import jax
import jax.numpy as jnp

CX = 16
CY = 32
CZ = 256
SURF_DEV = 2048
LONGWISE_NODES = 256
TRANSVERSE_NODES = 128
VERTICAL_NODES = 1024
DEVICE_COUNT = 256
SLOTS = 524288
SLAB = 114688
NPAR = 1835008
N_GY = 4
N_GZ = 4


def draw_boundary_voxel_locator(key, part):
    brick_cells = CX * CY * CZ
    brick_keys = jax.random.split(jax.random.fold_in(key, 17), DEVICE_COUNT)

    def one_brick(brick_key):
        shuffled = jax.random.permutation(brick_key, jnp.arange(brick_cells, dtype=jnp.int32))
        return jnp.sort(shuffled[:SURF_DEV]).astype(jnp.int32)
    return jax.vmap(one_brick)(brick_keys).reshape(SLOTS).astype(jnp.int32)


def draw_boundary_conductance_locator(key, part):
    device = jnp.arange(SLOTS, dtype=jnp.int32) // SURF_DEV
    block_x = device // (N_GY * N_GZ)
    return block_x * SLAB + jax.random.randint(key, (SLOTS,), 0, SLAB, dtype=jnp.int32)


def draw_boundary_active_entries(key, part):
    first_key, second_key = jax.random.split(key)
    counts = jax.random.randint(first_key, (DEVICE_COUNT,), SURF_DEV // 2, SURF_DEV + 1, dtype=jnp.int32)
    busiest = jax.random.randint(second_key, (), 0, DEVICE_COUNT, dtype=jnp.int32)
    return jnp.where(jnp.arange(DEVICE_COUNT, dtype=jnp.int32) == busiest, SURF_DEV, counts).astype(jnp.int32)


def with_ends(drawn, rng, least, high):
    longest = drawn.shape.index(max(drawn.shape))
    spots = []
    for shift in (0, 1):
        where = [jax.random.randint(jax.random.fold_in(rng, axis), (), 0, length) for axis, length in enumerate(drawn.shape)]
        where[longest] = (where[longest] + shift) % drawn.shape[longest]
        spots.append(tuple(where))
    return drawn.at[spots[0]].set(least).at[spots[1]].set(high)


def levels(own_key, extent, cuts, least, high):
    def one(dim, shards_of):
        steps = jax.random.uniform(jax.random.fold_in(jax.random.fold_in(own_key, 6), dim), (shards_of,), jnp.float32, least / len(cuts), high / len(cuts))
        return jnp.repeat(jnp.exp(steps), extent[dim] // shards_of).reshape((-1,) + (1,) * (len(extent) - dim - 1))

    level = one(*cuts[0])
    for cut in cuts[1:]:
        level = level * one(*cut)
    return level


def scatter_about(key, dims, spread, limit, cuts=(), kind=jnp.bfloat16):
    result = spread * jax.random.normal(key, dims, jnp.float32)
    if cuts:
        result = result * levels(key, dims, cuts, -0.22, 0.18)
    return jnp.clip(result, -limit, limit).astype(kind)


def setup_inputs(seed: int = 0) -> dict:
    keys = jax.random.split(jax.random.key(seed), 12)
    return {
        "saved_thermal_values": scatter_about(keys[0], (LONGWISE_NODES, TRANSVERSE_NODES, VERTICAL_NODES), 1.0, 4.0, ((0, 16), (1, 4), (2, 4)), jnp.float32),
        "saved_transformed_share": jnp.clip(0.9 * jax.random.uniform(keys[1], (LONGWISE_NODES, TRANSVERSE_NODES, VERTICAL_NODES), jnp.float32) ** levels(keys[1], (LONGWISE_NODES, TRANSVERSE_NODES, VERTICAL_NODES), ((0, 16), (1, 4), (2, 4)), -0.2, 0.2), 0.0, 0.9),
        "diffusion_numbers": jnp.clip(jnp.exp(math.log(0.15) - 1.3217559 * jax.random.uniform(keys[2], (LONGWISE_NODES, TRANSVERSE_NODES, VERTICAL_NODES), jnp.float32) ** levels(keys[2], (LONGWISE_NODES, TRANSVERSE_NODES, VERTICAL_NODES), ((0, 16), (1, 4), (2, 4)), -0.2, 0.2)), 0.04, 0.15),
        "transformation_status": with_ends(jax.random.randint(keys[3], (LONGWISE_NODES, TRANSVERSE_NODES, VERTICAL_NODES), 0, 3), jax.random.fold_in(keys[3], 1), 0, 2).astype(jnp.int32),
        "boundary_conductances": jnp.clip(jnp.exp(math.log(0.2) - 2.3025851 * jax.random.uniform(keys[4], (NPAR,), jnp.float32) ** levels(keys[4], (NPAR,), ((0, 256),), -0.2, 0.2)), 0.02, 0.2),
        "boundary_voxel_locator": draw_boundary_voxel_locator(jax.random.fold_in(keys[11], 71), 0),
        "boundary_conductance_locator": draw_boundary_conductance_locator(jax.random.fold_in(keys[11], 71), 0),
        "boundary_patch_extent": jnp.clip(0.5 + 1.0 * jax.random.uniform(keys[7], (SLOTS,), jnp.float32) ** levels(keys[7], (SLOTS,), ((0, 256),), -0.2, 0.2), 0.5, 1.5),
        "boundary_active_entries": draw_boundary_active_entries(jax.random.fold_in(keys[11], 71), 0),
        "thermal_error_factor": scatter_about(keys[9], (LONGWISE_NODES, TRANSVERSE_NODES, VERTICAL_NODES), 1.0, 6.0, ((0, 16), (1, 4), (2, 4)), jnp.float32),
        "product_error_factor": scatter_about(keys[10], (LONGWISE_NODES, TRANSVERSE_NODES, VERTICAL_NODES), 1.0, 6.0, ((0, 16), (1, 4), (2, 4)), jnp.float32),
    }


sharpness = 4.0
onset_temp = 0.0
kinetic_fast = 0.6
kinetic_slow = 0.2
enthalpy_release = 0.4
bath_thermal_level = -2.0

def adjacent_values(grid_field):
    padded = jnp.pad(grid_field, 1)
    total = padded[2:, 1:-1, 1:-1] + padded[:-2, 1:-1, 1:-1]
    total = total + padded[1:-1, 2:, 1:-1] + padded[1:-1, :-2, 1:-1]
    total = total + padded[1:-1, 1:-1, 2:] + padded[1:-1, 1:-1, :-2]
    return total

def march_forward_once(present_thermal_values, frac_now, diffusion_numbers, transformation_speed, thermal_drain_grid):
    gate_value = jax.nn.sigmoid(sharpness * (onset_temp - present_thermal_values))
    product_increase = transformation_speed * (1.0 - frac_now) * gate_value
    new_frac = frac_now + product_increase
    updated_thermal_values = present_thermal_values + diffusion_numbers * (adjacent_values(present_thermal_values) - 6.0 * present_thermal_values) + enthalpy_release * product_increase - thermal_drain_grid * (present_thermal_values - bath_thermal_level)
    return (updated_thermal_values, new_frac)

def reference(saved_thermal_values, saved_transformed_share, diffusion_numbers, transformation_status, boundary_conductances, boundary_voxel_locator, boundary_conductance_locator, boundary_patch_extent, boundary_active_entries, thermal_error_factor, product_error_factor):
    transformation_speed = kinetic_fast * (transformation_status == 1).astype(jnp.float32) + kinetic_slow * (transformation_status == 2).astype(jnp.float32)
    slot_index = jnp.arange(SLOTS, dtype=jnp.int32)
    device = slot_index // SURF_DEV
    local_slot = slot_index % SURF_DEV
    alive_slot = (local_slot < boundary_active_entries[device]).astype(jnp.float32)
    block_x = device // (N_GY * N_GZ)
    block_y = device // N_GZ % N_GY
    block_z = device % N_GZ
    cell_x = block_x * CX + boundary_voxel_locator // (CY * CZ)
    cell_y = block_y * CY + boundary_voxel_locator // CZ % CY
    cell_z = block_z * CZ + boundary_voxel_locator % CZ
    flat_cell = ((cell_x * TRANSVERSE_NODES + cell_y) * VERTICAL_NODES + cell_z).astype(jnp.int32)
    weight = alive_slot * boundary_patch_extent

    def forward(coef_values):
        thermal_drain_grid = jnp.zeros((LONGWISE_NODES * TRANSVERSE_NODES * VERTICAL_NODES,), jnp.float32).at[flat_cell].add(weight * coef_values[boundary_conductance_locator]).reshape(LONGWISE_NODES, TRANSVERSE_NODES, VERTICAL_NODES)
        thermal_values_next, transformed_share_next = march_forward_once(saved_thermal_values, saved_transformed_share, diffusion_numbers, transformation_speed, thermal_drain_grid)
        return march_forward_once(thermal_values_next, transformed_share_next, diffusion_numbers, transformation_speed, thermal_drain_grid)
    (temp_two, frac_two), reverse_mapping = jax.vjp(forward, boundary_conductances)
    transfer_sensitivity, = reverse_mapping((thermal_error_factor, product_error_factor))
    return (temp_two, frac_two, transfer_sensitivity)
```

```python
import functools

import jax
import jax.numpy as jnp
from jax import lax
from jax.experimental import pallas as pl
from jax.experimental.pallas import tpu as pltpu
from jax.sharding import PartitionSpec as P

MESH = pl.DeviceIdType.MESH
F32 = jnp.float32
BF16 = jnp.bfloat16
I32 = jnp.int32

NX, NY, NZ = 16, 32, 256
ROWS = NX * NY
SLOTS = 2048
CHUNK = 7168
CROWS = CHUNK // 128
HROWS = 4 * CROWS
SLAB = 16 * CHUNK
STEP = 512

sharpness = 4.0
kinetic_fast = 0.6
kinetic_slow = 0.2
enthalpy = 0.4
bath = -2.0


def halves(x):
    high = x.astype(BF16)
    return high, (x - high.astype(F32)).astype(BF16)


def one_hot(index, column, size):
    column = jnp.concatenate([column] * (index.shape[1] // 128), axis=1)
    hit = column == jnp.broadcast_to(index, (size, index.shape[1]))
    return jnp.where(hit, jnp.ones((), BF16), jnp.zeros((), BF16))


def row_hit(index, size):
    rows = lax.broadcasted_iota(I32, (size, index.shape[1]), 0)
    return rows == index


def gate(t):
    return jax.nn.sigmoid(sharpness * (0.0 - t))


def rate(status):
    return jnp.where(status == 1, kinetic_fast, jnp.where(status == 2, kinetic_slow, 0.0))


def steps(count, body):
    @pl.loop(0, count)
    def _(k):
        body(pl.ds(pl.multiple_of(k * STEP, STEP), STEP))


def decode(loc, gx, zh):
    local = loc - gx * SLAB
    row = local >> 7
    owner = (row * 1171) >> 16
    inner = row - owner * CROWS
    mine = ((owner >> 1) & 1) == zh
    return jnp.where(mine, (owner >> 2) * CROWS + inner, -1), (owner & 1) * 128 + (local & 127)


def neighbours(center, low, high, y_low, y_high, z_edge):
    y = lax.broadcasted_iota(I32, (NY, NZ), 0)
    z = lax.broadcasted_iota(I32, (NY, NZ), 1)
    edge = jnp.concatenate([z_edge, z_edge], axis=1)
    total = low + high
    total = total + jnp.where(y == 0, y_low, pltpu.roll(center, 1, 0))
    total = total + jnp.where(y == NY - 1, y_high, pltpu.roll(center, NY - 1, 0))
    total = total + jnp.where(z == 0, edge, pltpu.roll(center, 1, 1))
    return total + jnp.where(z == NZ - 1, edge, pltpu.roll(center, NZ - 1, 1))


def z_faces(x):
    x = x.reshape(ROWS, NZ)
    lane = lax.broadcasted_iota(I32, (ROWS, 128), 1)
    both = jnp.where(lane == 0, x[:, :128], x[:, 128:]).T
    return both[0:1, :], both[127:128, :]


def z_block(left, right):
    row = lax.broadcasted_iota(I32, (128, ROWS), 0)
    both = jnp.where(row == 0, left, jnp.where(row == 127, right, 0.0))
    return both.T.reshape(NX, NY, 128)


def kernel(
    active,
    t0_hbm,
    f0_hbm,
    dn_hbm,
    st_hbm,
    coef_hbm,
    cell_hbm,
    loc_hbm,
    ext_hbm,
    te_hbm,
    pe_hbm,
    temp_out,
    frac_out,
    sens_out,
    t0p,
    wp,
    t1p,
    f0,
    dn,
    st,
    te,
    pe,
    tb,
    f1,
    bf,
    cf,
    t2,
    f2,
    tab,
    rs,
    spread,
    sens,
    cell,
    loc,
    ploc,
    ext,
    lane_c,
    row_c,
    lane_a,
    row_a,
    lane_b,
    row_b,
    val_a,
    val_b,
    ret,
    sg,
    psg,
    ys,
    yr,
    ys1,
    yr1,
    zs,
    zr,
    zs1,
    zr1,
    zt,
    gfield,
    sink,
    acc,
    tmat,
    gmat,
    oh_lane,
    column,
    load_sem,
    send_sem,
    recv_sem,
    out_sem,
):
    gx, gy, gz = lax.axis_index("gx"), lax.axis_index("gy"), lax.axis_index("gz")
    zh, c = gz // 2, gz % 2
    even = c == 0
    outer_live = jnp.logical_or(gz == 1, gz == 2)
    partner = (gx, gy, 3 - gz)
    mate = (gx, gy, zh * 2 + (1 - c))
    x_up, x_down = (lax.rem(gx + 1, 16), gy, gz), (lax.rem(gx + 15, 16), gy, gz)
    y_up, y_down = (gx, lax.rem(gy + 1, 4), gz), (gx, lax.rem(gy + 3, 4), gz)
    peers = []
    for j in range(1, 8):
        pgy, pc = lax.rem(gy + j // 2, 4), lax.rem(c + j % 2, 2)
        peers.append((j, pgy, pc, (gx, pgy, zh * 2 + pc)))

    barrier = pltpu.get_barrier_semaphore()
    met = [x_up, x_down, partner] + [p[3] for p in peers]
    for device in met:
        pl.semaphore_signal(barrier, inc=1, device_id=device, device_id_type=MESH)

    loads = {}
    for k, (name, source, target) in enumerate(
        (
            ("t0", t0_hbm, t0p.at[pl.ds(1, NX)]),
            ("dn", dn_hbm, dn),
            ("te", te_hbm, te),
            ("cell", cell_hbm, cell),
            ("loc", loc_hbm, loc),
            ("ext", ext_hbm, ext),
            ("coef", coef_hbm, tab.at[gy, c]),
            ("f0", f0_hbm, f0),
            ("st", st_hbm, st),
            ("pe", pe_hbm, pe),
        )
    ):
        loads[name] = pltpu.make_async_copy(source, target, load_sem.at[k])
        loads[name].start()

    sent = []

    def send(source, target, index, device):
        copy = pltpu.make_async_remote_copy(
            src_ref=source,
            dst_ref=target,
            send_sem=send_sem.at[index],
            recv_sem=recv_sem.at[index],
            device_id=device,
            device_id_type=MESH,
        )
        copy.start()
        sent.append(copy)
        return copy

    base = lax.broadcasted_iota(I32, (256, 128), 0).astype(F32).astype(BF16)
    column[...] = base

    loads["t0"].wait()
    loads["dn"].wait()
    loads["te"].wait()

    @pl.loop(0, NX)
    def _(i):
        wp[i + 1] = dn[i] * te[i]

    for k, padded in enumerate((t0p, wp)):
        ys[0, k] = padded[1:17, 0:1, :]
        ys[1, k] = padded[1:17, NY - 1 : NY, :]
        left, right = z_faces(padded[1:17])
        zs[0, k : k + 1] = jnp.where(even, right, left)
        zs[1, k : k + 1] = jnp.where(even, left, right)

    pl.semaphore_wait(barrier, len(met))

    to_partner = send(loc_hbm, ploc, 0, partner)
    table = [send(coef_hbm, tab.at[gy, c], j, device) for j, _, _, device in peers]
    halo = [
        send(zs.at[1], zr.at[1], 8, partner),
        send(zs.at[0], zr.at[0], 9, mate),
        send(t0p.at[1], t0p.at[NX + 1], 10, x_down),
        send(t0p.at[NX], t0p.at[0], 11, x_up),
        send(wp.at[1], wp.at[NX + 1], 12, x_down),
        send(wp.at[NX], wp.at[0], 13, x_up),
        send(ys.at[0], yr.at[1], 14, y_down),
        send(ys.at[1], yr.at[0], 15, y_up),
    ]

    for name in ("cell", "loc", "ext"):
        loads[name].wait()
    lane_c[...] = (cell[...] & (NZ - 1)).astype(F32)
    row_c[...] = cell[...] >> 8
    row, lane = decode(loc[...], gx, zh)
    row_a[...], lane_a[...] = row, lane.astype(F32)
    slot = lax.broadcasted_iota(I32, (1, SLOTS), 1)
    ext[...] = jnp.where(slot < active[0], ext[...], 0.0)

    def make_cells(cols):
        oh_lane[:, cols] = one_hot(lane_c[:, cols].astype(BF16), column[...], NZ)

    steps(SLOTS // STEP, make_cells)
    for name in ("f0", "st", "pe"):
        loads[name].wait()

    for copy in halo:
        copy.wait_recv()
    for padded in (t0p, wp):
        padded[0] = jnp.where(gx > 0, padded[0], 0.0)
        padded[NX + 1] = jnp.where(gx < 15, padded[NX + 1], 0.0)
    yr[0] = jnp.where(gy > 0, yr[0], 0.0)
    yr[1] = jnp.where(gy < 3, yr[1], 0.0)

    def z_halo(inner, outer):
        outer = jnp.where(outer_live, outer, 0.0)
        return z_block(jnp.where(even, outer, inner), jnp.where(even, inner, outer))

    for k in range(2):
        zt[k] = z_halo(zr[0, k : k + 1], zr[1, k : k + 1])

    @pl.loop(0, NX)
    def _(i):
        t = t0p[i + 1]
        around = neighbours(t, t0p[i], t0p[i + 2], yr[0, 0, i], yr[1, 0, i], zt[0, i])
        adjoint = neighbours(wp[i + 1], wp[i], wp[i + 2], yr[0, 1, i], yr[1, 1, i], zt[1, i])
        d, tw = dn[i], te[i]
        growth = rate(st[i]) * (1.0 - f0[i]) * gate(t)
        tb[i] = t + d * (around - 6.0 * t) + enthalpy * growth
        new = f0[i] + growth
        f1[i] = new
        bf[i] = tw * (1.0 - 6.0 * d) + adjoint
        cf[i] = (enthalpy * tw + pe[i]) * (rate(st[i]) * (1.0 - new)) * -sharpness

    def gather(matrix, size, lane_ref, row_ref, out, stored=None):
        def chunk(cols):
            if stored is None:
                hot = one_hot(lane_ref[:, cols].astype(BF16), column[...], 256)
            else:
                hot = stored[:, cols]
            found = jnp.dot(
                matrix[...],
                jnp.concatenate([hot, hot], axis=0),
                preferred_element_type=F32,
            )
            found = jnp.where(row_hit(row_ref[:, cols], size), found, 0.0)
            out[:, cols] = jnp.sum(found, axis=0, keepdims=True)

        steps(SLOTS // STEP, chunk)

    def scatter(value, size, lane_ref, row_ref, out, stored=None):
        def chunk(cols):
            if stored is None:
                hot = one_hot(lane_ref[:, cols].astype(BF16), column[...], 256)
            else:
                hot = stored[:, cols]
            high, low = halves(value[:, cols])
            right = jnp.concatenate(
                [hot * jnp.broadcast_to(high, hot.shape), hot * jnp.broadcast_to(low, hot.shape)],
                axis=1,
            )
            left = jnp.where(row_hit(row_ref[:, cols], size), 1.0, 0.0).astype(BF16)
            out[...] += lax.dot_general(
                jnp.concatenate([left, left], axis=1),
                right,
                (((1,), (1,)), ((), ())),
                preferred_element_type=F32,
            )

        steps(SLOTS // STEP, chunk)

    loads["coef"].wait()
    to_partner.wait_recv()
    for copy in table:
        copy.wait_recv()
    row, lane = decode(ploc[...], gx, zh)
    row_b[...], lane_b[...] = row, lane.astype(F32)
    pieces = []
    for part in range(2):
        pieces.append(halves(tab[:, part].reshape(HROWS, 128)))
    tmat[...] = jnp.concatenate(
        [pieces[0][0], pieces[1][0], pieces[0][1], pieces[1][1]], axis=1
    )
    gather(tmat, HROWS, lane_b, row_b, val_b)
    reply = send(val_b, ret, 16, partner)
    gather(tmat, HROWS, lane_a, row_a, val_a)
    reply.wait_recv()
    val_a[...] = ext[...] * (val_a[...] + ret[...])
    sink[...] = jnp.zeros_like(sink)
    scatter(val_a, ROWS, lane_c, row_c, sink, oh_lane)

    @pl.loop(0, NX)
    def _(i):
        rows = pl.ds(pl.multiple_of(i * NY, NY), NY)
        t, drain, tw, d = t0p[i + 1], sink[rows, :], te[i], dn[i]
        lifted = t - bath
        t1 = tb[i] - drain * lifted
        t1p[i + 1] = t1
        g = gate(t1)
        growth = rate(st[i]) * (1.0 - f1[i]) * g
        f2[i] = f1[i] + growth
        t2[i] = t1 - 6.0 * d * t1 + enthalpy * growth - drain * (t1 - bath)
        dual = bf[i] - tw * drain + cf[i] * g * (1.0 - g)
        high, low = halves(-(tw * (t1 - bath) + dual * lifted))
        gmat[rows, 0:NZ] = high
        gmat[rows, NZ : 2 * NZ] = low

    frac_copy = pltpu.make_async_copy(f2, frac_out, out_sem.at[0])
    frac_copy.start()
    gather(gmat, ROWS, lane_c, row_c, sg, oh_lane)
    sg[...] = ext[...] * sg[...]
    slots = send(sg, psg, 17, partner)

    ys1[0] = t1p[1:17, 0:1, :]
    ys1[1] = t1p[1:17, NY - 1 : NY, :]
    left, right = z_faces(t1p[1:17])
    zs1[0] = jnp.where(even, right, left)
    zs1[1] = jnp.where(even, left, right)
    halo = [
        send(zs1.at[1], zr1.at[1], 18, partner),
        send(zs1.at[0], zr1.at[0], 19, mate),
        send(t1p.at[1], t1p.at[NX + 1], 20, x_down),
        send(t1p.at[NX], t1p.at[0], 21, x_up),
        send(ys1.at[0], yr1.at[1], 22, y_down),
        send(ys1.at[1], yr1.at[0], 23, y_up),
    ]
    acc[...] = jnp.zeros_like(acc)
    scatter(sg, HROWS, lane_a, row_a, acc)
    slots.wait_recv()
    scatter(psg, HROWS, lane_b, row_b, acc)
    for g in range(4):
        for part in range(2):
            spread[g, part] = acc[g * CROWS : (g + 1) * CROWS, part * 128 : (part + 1) * 128]
    shares = [
        send(spread.at[pgy, pc], rs.at[j], 23 + j, device) for j, pgy, pc, device in peers
    ]

    for copy in halo:
        copy.wait_recv()
    t1p[0] = jnp.where(gx > 0, t1p[0], 0.0)
    t1p[NX + 1] = jnp.where(gx < 15, t1p[NX + 1], 0.0)
    yr1[0] = jnp.where(gy > 0, yr1[0], 0.0)
    yr1[1] = jnp.where(gy < 3, yr1[1], 0.0)
    zt[0] = z_halo(zr1[0], zr1[1])

    @pl.loop(0, NX)
    def _(i):
        around = neighbours(
            t1p[i + 1], t1p[i], t1p[i + 2], yr1[0, i], yr1[1, i], zt[0, i]
        )
        t2[i] = t2[i] + dn[i] * around

    temp_copy = pltpu.make_async_copy(t2, temp_out, out_sem.at[1])
    temp_copy.start()
    total = spread[gy, c]
    for copy, (j, _, _, _) in zip(shares, peers):
        copy.wait_recv()
        total = total + rs[j]
    sens[...] = total
    sens_copy = pltpu.make_async_copy(sens, sens_out, out_sem.at[2])
    sens_copy.start()
    for copy in sent:
        copy.wait_send()
    frac_copy.wait()
    temp_copy.wait()
    sens_copy.wait()


def on_device(t0, f0, dn, st, coef, cell, loc, ext, active, te, pe):
    field = (NX, NY, NZ)
    padded = (NX + 2, NY, NZ)
    row = (1, SLOTS)
    vmem = pltpu.VMEM
    anywhere = pl.BlockSpec(memory_space=pl.ANY)
    scratch = (
        [vmem(padded, F32)] * 3
        + [vmem(field, F32)] * 2
        + [vmem(field, I32)]
        + [vmem(field, F32)] * 8
        + [
            vmem((4, 2, CROWS, 128), F32),
            vmem((8, CROWS, 128), F32),
            vmem((4, 2, CROWS, 128), F32),
            vmem((CROWS, 128), F32),
            vmem(row, I32),
            vmem(row, I32),
            vmem(row, I32),
            vmem(row, F32),
        ]
        + [vmem(row, F32), vmem(row, I32)] * 3
        + [vmem(row, F32)] * 5
        + [vmem((2, 2, NX, 1, NZ), F32)] * 2
        + [vmem((2, NX, 1, NZ), F32)] * 2
        + [vmem((2, 2, ROWS), F32)] * 2
        + [vmem((2, 1, ROWS), F32)] * 2
        + [
            vmem((2, NX, NY, 128), F32),
            vmem((8, 128), F32),
            vmem((ROWS, NZ), F32),
            vmem((HROWS, 256), F32),
            vmem((HROWS, 512), BF16),
            vmem((ROWS, 512), BF16),
            vmem((NZ, SLOTS), BF16),
            vmem((256, 128), BF16),
            pltpu.SemaphoreType.DMA((10,)),
            pltpu.SemaphoreType.DMA((31,)),
            pltpu.SemaphoreType.DMA((31,)),
            pltpu.SemaphoreType.DMA((3,)),
        ]
    )
    temp, frac, sens = pl.pallas_call(
        kernel,
        out_shape=(
            jax.ShapeDtypeStruct(field, F32),
            jax.ShapeDtypeStruct(field, F32),
            jax.ShapeDtypeStruct((CROWS, 128), F32),
        ),
        in_specs=[pl.BlockSpec(memory_space=pltpu.SMEM)] + [anywhere] * 10,
        out_specs=(anywhere,) * 3,
        scratch_shapes=scratch,
        compiler_params=pltpu.CompilerParams(
            collective_id=0, has_side_effects=True, vmem_limit_bytes=56 * 2**20
        ),
    )(
        active,
        t0,
        f0,
        dn,
        st,
        coef.reshape(CROWS, 128),
        cell.reshape(row),
        loc.reshape(row),
        ext.reshape(row),
        te,
        pe,
    )
    return temp, frac, sens.reshape(CHUNK)


def solution(mesh):
    brick, line = P("gx", "gy", "gz"), P(("gx", "gy", "gz"))
    return jax.shard_map(
        on_device,
        mesh=mesh,
        in_specs=(brick,) * 4 + (line,) * 5 + (brick,) * 2,
        out_specs=(brick, brick, line),
        check_vma=False,
    )
```

```python
import functools

import jax
import jax.numpy as jnp
from jax import lax
from jax.experimental import pallas as pl
from jax.experimental.pallas import tpu as pltpu
from jax.sharding import PartitionSpec as P

MESH = pl.DeviceIdType.MESH
F32 = jnp.float32
BF16 = jnp.bfloat16
I32 = jnp.int32

NX, NY, NZ = 16, 32, 256
ROWS = NX * NY
SLOTS = 2048
CHUNK = 7168
CROWS = CHUNK // 128
HROWS = 4 * CROWS
SLAB = 16 * CHUNK

sharpness = 4.0
kinetic_fast = 0.6
kinetic_slow = 0.2
enthalpy = 0.4
bath = -2.0


def halves(x):
    high = x.astype(BF16)
    return high, (x - high.astype(F32)).astype(BF16)


def one_hot(index, column, size):
    column = jnp.concatenate([column] * (index.shape[1] // 128), axis=1)
    hit = column == jnp.broadcast_to(index, (size, index.shape[1]))
    return jnp.where(hit, jnp.ones((), BF16), jnp.zeros((), BF16))


def row_hit(index, size):
    rows = lax.broadcasted_iota(I32, (size, index.shape[1]), 0)
    return rows == index


def gate(t):
    return jax.nn.sigmoid(sharpness * (0.0 - t))


def rate(status):
    return jnp.where(status == 1, kinetic_fast, jnp.where(status == 2, kinetic_slow, 0.0))


def decode(loc, gx, zh):
    local = loc - gx * SLAB
    row = local >> 7
    owner = (row * 1171) >> 16
    inner = row - owner * CROWS
    mine = ((owner >> 1) & 1) == zh
    return jnp.where(mine, (owner >> 2) * CROWS + inner, -1), (owner & 1) * 128 + (local & 127)


def neighbours(center, low, high, y_low, y_high, z_edge):
    y = lax.broadcasted_iota(I32, (NY, NZ), 0)
    z = lax.broadcasted_iota(I32, (NY, NZ), 1)
    edge = jnp.concatenate([z_edge, z_edge], axis=1)
    total = low + high
    total = total + jnp.where(y == 0, y_low, pltpu.roll(center, 1, 0))
    total = total + jnp.where(y == NY - 1, y_high, pltpu.roll(center, NY - 1, 0))
    total = total + jnp.where(z == 0, edge, pltpu.roll(center, 1, 1))
    return total + jnp.where(z == NZ - 1, edge, pltpu.roll(center, NZ - 1, 1))


def z_faces(x):
    x = x.reshape(ROWS, NZ)
    lane = lax.broadcasted_iota(I32, (ROWS, 128), 1)
    both = jnp.where(lane == 0, x[:, :128], x[:, 128:]).T
    return both[0:1, :], both[127:128, :]


def z_block(left, right):
    row = lax.broadcasted_iota(I32, (128, ROWS), 0)
    both = jnp.where(row == 0, left, jnp.where(row == 127, right, 0.0))
    return both.T.reshape(NX, NY, 128)


def kernel(
    active,
    t0_hbm,
    f0_hbm,
    dn_hbm,
    st_hbm,
    coef_hbm,
    cell_hbm,
    loc_hbm,
    ext_hbm,
    te_hbm,
    pe_hbm,
    t2,
    f2,
    sens,
    t0p,
    wp,
    t1p,
    f0,
    dn,
    st,
    te,
    pe,
    tb,
    f1,
    tab,
    rs,
    spread,
    cell,
    loc,
    ploc,
    ext,
    row_c,
    lane_a,
    row_a,
    lane_b,
    row_b,
    val_a,
    val_b,
    ret,
    sg,
    psg,
    ys,
    yr,
    ys1,
    yr1,
    zs,
    zr,
    zs1,
    zr1,
    zt,
    sink,
    acc,
    tmat,
    fmat,
    fv,
    oh_lane,
    column,
    load_sem,
    send_sem,
    recv_sem,
):
    gx, gy, gz = lax.axis_index("gx"), lax.axis_index("gy"), lax.axis_index("gz")
    zh, c = gz // 2, gz % 2
    even = c == 0
    outer_live = jnp.logical_or(gz == 1, gz == 2)
    partner = (gx, gy, 3 - gz)
    mate = (gx, gy, zh * 2 + (1 - c))
    x_up, x_down = (jnp.minimum(gx + 1, 15), gy, gz), (jnp.maximum(gx - 1, 0), gy, gz)
    has_up, has_down = gx < 15, gx > 0
    first, second = zh == 0, zh == 1
    y_up, y_down = (gx, lax.rem(gy + 1, 4), gz), (gx, lax.rem(gy + 3, 4), gz)
    peers = []
    for j in range(1, 8):
        pgy, pc = lax.rem(gy + j // 2, 4), lax.rem(c + j % 2, 2)
        peers.append((j, pgy, pc, (gx, pgy, zh * 2 + pc)))

    barrier = pltpu.get_barrier_semaphore()

    def greet(device):
        pl.semaphore_signal(barrier, inc=1, device_id=device, device_id_type=MESH)

    pl.when(first)(lambda: greet(partner))
    pl.when(has_up)(lambda: greet(x_up))
    pl.when(has_down)(lambda: greet(x_down))
    for _, _, _, device in peers:
        greet(device)
    expected = 7 + has_up.astype(I32) + has_down.astype(I32) + zh

    loads = {}
    for k, (name, source, target) in enumerate(
        (
            ("t0", t0_hbm, t0p.at[pl.ds(1, NX)]),
            ("dn", dn_hbm, dn),
            ("te", te_hbm, te),
            ("cell", cell_hbm, cell),
            ("loc", loc_hbm, loc),
            ("ext", ext_hbm, ext),
            ("coef", coef_hbm, tab.at[gy, c]),
            ("f0", f0_hbm, f0),
            ("st", st_hbm, st),
            ("pe", pe_hbm, pe),
        )
    ):
        loads[name] = pltpu.make_async_copy(source, target, load_sem.at[k])
        loads[name].start()

    sent = []

    def remote(source, target, index, device):
        return pltpu.make_async_remote_copy(
            src_ref=source,
            dst_ref=target,
            send_sem=send_sem.at[index],
            recv_sem=recv_sem.at[index],
            device_id=device,
            device_id_type=MESH,
        )

    def send(source, target, index, device):
        copy = remote(source, target, index, device)
        copy.start()
        sent.append(copy.wait_send)
        return copy

    def send_x(padded, index):
        down = remote(padded.at[1], padded.at[NX + 1], index, x_down)
        up = remote(padded.at[NX], padded.at[0], index + 1, x_up)
        pl.when(has_down)(down.start)
        pl.when(has_up)(up.start)
        sent.append(lambda: pl.when(has_down)(down.wait_send))
        sent.append(lambda: pl.when(has_up)(up.wait_send))

        def arrived():
            pl.when(has_up)(down.wait_recv)
            pl.when(has_down)(up.wait_recv)
            padded[0] = jnp.where(has_down, padded[0], 0.0)
            padded[NX + 1] = jnp.where(has_up, padded[NX + 1], 0.0)

        return arrived

    base = lax.broadcasted_iota(I32, (256, 128), 0).astype(F32).astype(BF16)
    column[...] = base

    loads["t0"].wait()
    loads["dn"].wait()
    loads["te"].wait()

    @pl.loop(0, NX)
    def _(i):
        wp[i + 1] = dn[i] * te[i]

    for k, padded in enumerate((t0p, wp)):
        ys[0, k] = padded[1:17, 0:1, :]
        ys[1, k] = padded[1:17, NY - 1 : NY, :]
        left, right = z_faces(padded[1:17])
        zs[0, k : k + 1] = jnp.where(even, right, left)
        zs[1, k : k + 1] = jnp.where(even, left, right)

    pl.semaphore_wait(barrier, expected)
    table = [send(coef_hbm, tab.at[gy, c], j, device) for j, _, _, device in peers]
    request = remote(loc_hbm, ploc, 0, partner)
    outer = remote(zs.at[1], zr.at[1], 8, partner)

    def ask():
        request.start()
        outer.start()

    pl.when(second)(ask)
    halo = [
        send(zs.at[0], zr.at[0], 9, mate),
        send(ys.at[0], yr.at[1], 14, y_down),
        send(ys.at[1], yr.at[0], 15, y_up),
    ]
    halo_x = [send_x(t0p, 10), send_x(wp, 12)]
    sent.append(request.wait_send)
    sent.append(outer.wait_send)

    for name in ("cell", "loc", "ext"):
        loads[name].wait()
    cell_row = cell[...] >> 8
    oh_lane[...] = one_hot((cell[...] & (NZ - 1)).astype(F32).astype(BF16), column[...], NZ)
    row_c[...] = cell_row
    row, lane = decode(loc[...], gx, zh)
    row_a[...], lane_a[...] = row, lane.astype(F32)
    slot = lax.broadcasted_iota(I32, (1, SLOTS), 1)
    ext[...] = jnp.where(slot < active[0], ext[...], 0.0)
    for name in ("f0", "st", "pe"):
        loads[name].wait()

    def put(k, rows, x):
        high, low = halves(x)
        fmat[k, rows, 0:NZ] = high
        fmat[k, rows, NZ : 2 * NZ] = low

    @pl.loop(0, NX)
    def _(i):
        rows = pl.ds(pl.multiple_of(i * NY, NY), NY)
        t, tw = t0p[i + 1], te[i]
        lifted = t - bath
        growth = rate(st[i]) * (1.0 - f0[i]) * gate(t)
        new = f0[i] + growth
        f1[i] = new
        tb[i] = enthalpy * growth
        slope = (enthalpy * tw + pe[i]) * (rate(st[i]) * (1.0 - new)) * -sharpness
        put(0, rows, lifted)
        put(1, rows, tw * lifted)
        put(2, rows, slope * lifted)

    def gather(matrix, size, hot, row, out):
        found = jnp.dot(
            matrix[...], jnp.concatenate([hot, hot], axis=0), preferred_element_type=F32
        )
        found = jnp.where(row_hit(row, size), found, 0.0)
        out[...] = jnp.sum(found, axis=0, keepdims=True)

    def scatter(value, size, hot, row):
        high, low = halves(value)
        right = jnp.concatenate(
            [hot * jnp.broadcast_to(high, hot.shape), hot * jnp.broadcast_to(low, hot.shape)],
            axis=1,
        )
        left = jnp.where(row_hit(row, size), 1.0, 0.0).astype(BF16)
        return lax.dot_general(
            jnp.concatenate([left, left], axis=1),
            right,
            (((1,), (1,)), ((), ())),
            preferred_element_type=F32,
        )

    def hot_lanes(ref):
        return one_hot(ref[...].astype(BF16), column[...], 256)

    for k in range(3):
        gather(fmat.at[k], ROWS, oh_lane[...], row_c[...], fv.at[k])

    loads["coef"].wait()
    for copy in table:
        copy.wait_recv()
    pieces = []
    for part in range(2):
        pieces.append(halves(tab[:, part].reshape(HROWS, 128)))
    tmat[...] = jnp.concatenate(
        [pieces[0][0], pieces[1][0], pieces[0][1], pieces[1][1]], axis=1
    )
    gather(tmat, HROWS, hot_lanes(lane_a), row_a[...], val_a)

    request.wait_recv()
    pl.when(first)(ask)
    row, lane = decode(ploc[...], gx, zh)
    row_b[...], lane_b[...] = row, lane.astype(F32)
    gather(tmat, HROWS, hot_lanes(lane_b), row_b[...], val_b)
    reply = send(val_b, ret, 16, partner)

    for copy in halo:
        copy.wait_recv()
    for arrived in halo_x:
        arrived()
    outer.wait_recv()
    yr[0] = jnp.where(gy > 0, yr[0], 0.0)
    yr[1] = jnp.where(gy < 3, yr[1], 0.0)

    def z_halo(inner, outer):
        outer = jnp.where(outer_live, outer, 0.0)
        return z_block(jnp.where(even, outer, inner), jnp.where(even, inner, outer))

    for k in range(2):
        zt[k] = z_halo(zr[0, k : k + 1], zr[1, k : k + 1])

    @pl.loop(0, NX)
    def _(i):
        t = t0p[i + 1]
        around = neighbours(t, t0p[i], t0p[i + 2], yr[0, 0, i], yr[1, 0, i], zt[0, i])
        adjoint = neighbours(wp[i + 1], wp[i], wp[i + 2], yr[0, 1, i], yr[1, 1, i], zt[1, i])
        d, tw = dn[i], te[i]
        rows = pl.ds(pl.multiple_of(i * NY, NY), NY)
        plain = t + d * (around - 6.0 * t) + tb[i]
        tb[i] = plain
        put(3, rows, plain)
        put(4, rows, tw * (plain - bath) + (tw * (1.0 - 6.0 * d) + adjoint) * (t - bath))

    for k in range(3, 5):
        gather(fmat.at[k], ROWS, oh_lane[...], row_c[...], fv.at[k])

    reply.wait_recv()
    drain = ext[...] * (val_a[...] + ret[...])
    val_a[...] = drain
    g = gate(fv[3] - drain * fv[0])
    sg[...] = -ext[...] * (fv[4] - 2.0 * drain * fv[1] + fv[2] * (g * (1.0 - g)))
    slots = send(sg, psg, 17, partner)
    sink[...] = scatter(val_a[...], ROWS, oh_lane[...], row_c[...])

    @pl.loop(0, NX)
    def _(i):
        rows = pl.ds(pl.multiple_of(i * NY, NY), NY)
        drain = sink[rows, :]
        t1 = tb[i] - drain * (t0p[i + 1] - bath)
        t1p[i + 1] = t1
        growth = rate(st[i]) * (1.0 - f1[i]) * gate(t1)
        f2[i] = f1[i] + growth
        t2[i] = t1 - 6.0 * dn[i] * t1 + enthalpy * growth - drain * (t1 - bath)

    ys1[0] = t1p[1:17, 0:1, :]
    ys1[1] = t1p[1:17, NY - 1 : NY, :]
    left, right = z_faces(t1p[1:17])
    zs1[0] = jnp.where(even, right, left)
    zs1[1] = jnp.where(even, left, right)
    halo = [
        send(zs1.at[1], zr1.at[1], 18, partner),
        send(zs1.at[0], zr1.at[0], 19, mate),
        send(ys1.at[0], yr1.at[1], 22, y_down),
        send(ys1.at[1], yr1.at[0], 23, y_up),
    ]
    halo_x = send_x(t1p, 20)
    acc[...] = scatter(sg[...], HROWS, hot_lanes(lane_a), row_a[...])
    slots.wait_recv()
    acc[...] += scatter(psg[...], HROWS, hot_lanes(lane_b), row_b[...])
    for g in range(4):
        for part in range(2):
            spread[g, part] = acc[g * CROWS : (g + 1) * CROWS, part * 128 : (part + 1) * 128]
    shares = [
        send(spread.at[pgy, pc], rs.at[j], 23 + j, device) for j, pgy, pc, device in peers
    ]

    for copy in halo:
        copy.wait_recv()
    halo_x()
    yr1[0] = jnp.where(gy > 0, yr1[0], 0.0)
    yr1[1] = jnp.where(gy < 3, yr1[1], 0.0)
    zt[0] = z_halo(zr1[0], zr1[1])

    @pl.loop(0, NX)
    def _(i):
        around = neighbours(
            t1p[i + 1], t1p[i], t1p[i + 2], yr1[0, i], yr1[1, i], zt[0, i]
        )
        t2[i] = t2[i] + dn[i] * around

    total = spread[gy, c]
    for copy, (j, _, _, _) in zip(shares, peers):
        copy.wait_recv()
        total = total + rs[j]
    sens[...] = total
    for wait in sent:
        wait()


def deliver(t2, f2, sens, temp_out, frac_out, sens_out, sem):
    copies = [
        pltpu.make_async_copy(source, target, sem.at[k])
        for k, (source, target) in enumerate(((t2, temp_out), (f2, frac_out), (sens, sens_out)))
    ]
    for copy in copies:
        copy.start()
    for copy in copies:
        copy.wait()


def on_device(t0, f0, dn, st, coef, cell, loc, ext, active, te, pe):
    field = (NX, NY, NZ)
    padded = (NX + 2, NY, NZ)
    row = (1, SLOTS)
    vmem = pltpu.VMEM
    anywhere = pl.BlockSpec(memory_space=pl.ANY)
    scratch = (
        [vmem(padded, F32)] * 3
        + [vmem(field, F32)] * 2
        + [vmem(field, I32)]
        + [vmem(field, F32)] * 4
        + [
            vmem((4, 2, CROWS, 128), F32),
            vmem((8, CROWS, 128), F32),
            vmem((4, 2, CROWS, 128), F32),
            vmem(row, I32),
            vmem(row, I32),
            vmem(row, I32),
            vmem(row, F32),
        ]
        + [vmem(row, I32)]
        + [vmem(row, F32), vmem(row, I32)] * 2
        + [vmem(row, F32)] * 5
        + [vmem((2, 2, NX, 1, NZ), F32)] * 2
        + [vmem((2, NX, 1, NZ), F32)] * 2
        + [vmem((2, 2, ROWS), F32)] * 2
        + [vmem((2, 1, ROWS), F32)] * 2
        + [
            vmem((2, NX, NY, 128), F32),
            vmem((ROWS, NZ), F32),
            vmem((HROWS, 256), F32),
            vmem((HROWS, 512), BF16),
            vmem((5, ROWS, 512), BF16),
            vmem((5, 1, SLOTS), F32),
            vmem((NZ, SLOTS), BF16),
            vmem((256, 128), BF16),
            pltpu.SemaphoreType.DMA((10,)),
            pltpu.SemaphoreType.DMA((31,)),
            pltpu.SemaphoreType.DMA((31,)),
        ]
    )
    results = (
        jax.ShapeDtypeStruct(field, F32),
        jax.ShapeDtypeStruct(field, F32),
        jax.ShapeDtypeStruct((CROWS, 128), F32),
    )
    done = pl.pallas_call(
        kernel,
        out_shape=results,
        in_specs=[pl.BlockSpec(memory_space=pltpu.SMEM)] + [anywhere] * 10,
        out_specs=(pl.BlockSpec(memory_space=vmem),) * 3,
        scratch_shapes=scratch,
        compiler_params=pltpu.CompilerParams(
            collective_id=0, has_side_effects=True, vmem_limit_bytes=56 * 2**20
        ),
    )(
        active,
        t0,
        f0,
        dn,
        st,
        coef.reshape(CROWS, 128),
        cell.reshape(row),
        loc.reshape(row),
        ext.reshape(row),
        te,
        pe,
    )
    temp, frac, sens = pl.pallas_call(
        deliver,
        out_shape=results,
        in_specs=[pl.BlockSpec(memory_space=vmem)] * 3,
        out_specs=(anywhere,) * 3,
        scratch_shapes=[pltpu.SemaphoreType.DMA((3,))],
    )(*done)
    return temp, frac, sens.reshape(CHUNK)


def solution(mesh):
    brick, line = P("gx", "gy", "gz"), P(("gx", "gy", "gz"))
    return jax.shard_map(
        on_device,
        mesh=mesh,
        in_specs=(brick,) * 4 + (line,) * 5 + (brick,) * 2,
        out_specs=(brick, brick, line),
        check_vma=False,
    )
```

```python
import functools

import jax
import jax.numpy as jnp
from jax import lax
from jax.experimental import pallas as pl
from jax.experimental.pallas import tpu as pltpu
from jax.sharding import PartitionSpec as P

MESH = pl.DeviceIdType.MESH
F32 = jnp.float32
BF16 = jnp.bfloat16
I32 = jnp.int32

NX, NY, NZ = 16, 32, 256
ROWS = NX * NY
SLOTS = 2048
CHUNK = 7168
CROWS = CHUNK // 128
HROWS = 4 * CROWS
SLAB = 16 * CHUNK
GROUP = 256
GROUPS = SLOTS // GROUP
WIDTH = 64
WINDOWS = ROWS // WIDTH
VISITS = GROUPS + WINDOWS - 1

sharpness = 4.0
kinetic_fast = 0.6
kinetic_slow = 0.2
enthalpy = 0.4
bath = -2.0


def halves(x):
    high = x.astype(BF16)
    return high, (x - high.astype(F32)).astype(BF16)


def one_hot(index, column, size):
    column = jnp.concatenate([column] * (index.shape[1] // 128), axis=1)
    hit = column == jnp.broadcast_to(index, (size, index.shape[1]))
    return jnp.where(hit, jnp.ones((), BF16), jnp.zeros((), BF16))


def row_hit(index, size):
    rows = lax.broadcasted_iota(I32, (size, index.shape[1]), 0)
    return rows == index


def gate(t):
    return jax.nn.sigmoid(sharpness * (0.0 - t))


def rate(status):
    return jnp.where(status == 1, kinetic_fast, jnp.where(status == 2, kinetic_slow, 0.0))


def decode(loc, gx, zh):
    local = loc - gx * SLAB
    row = local >> 7
    owner = (row * 1171) >> 16
    inner = row - owner * CROWS
    mine = ((owner >> 1) & 1) == zh
    return jnp.where(mine, (owner >> 2) * CROWS + inner, -1), (owner & 1) * 128 + (local & 127)


def neighbours(center, low, high, y_low, y_high, z_edge):
    y = lax.broadcasted_iota(I32, (NY, NZ), 0)
    z = lax.broadcasted_iota(I32, (NY, NZ), 1)
    edge = jnp.concatenate([z_edge, z_edge], axis=1)
    total = low + high
    total = total + jnp.where(y == 0, y_low, pltpu.roll(center, 1, 0))
    total = total + jnp.where(y == NY - 1, y_high, pltpu.roll(center, NY - 1, 0))
    total = total + jnp.where(z == 0, edge, pltpu.roll(center, 1, 1))
    return total + jnp.where(z == NZ - 1, edge, pltpu.roll(center, NZ - 1, 1))


def z_faces(x):
    x = x.reshape(ROWS, NZ)
    lane = lax.broadcasted_iota(I32, (ROWS, 128), 1)
    both = jnp.where(lane == 0, x[:, :128], x[:, 128:]).T
    return both[0:1, :], both[127:128, :]


def z_block(left, right):
    row = lax.broadcasted_iota(I32, (128, ROWS), 0)
    both = jnp.where(row == 0, left, jnp.where(row == 127, right, 0.0))
    return both.T.reshape(NX, NY, 128)


def kernel(
    active,
    t0_hbm,
    f0_hbm,
    dn_hbm,
    st_hbm,
    coef_hbm,
    cell_hbm,
    loc_hbm,
    ext_hbm,
    te_hbm,
    pe_hbm,
    temp_out,
    frac_out,
    sens_out,
    t0p,
    wp,
    t1p,
    f0,
    dn,
    st,
    te,
    pe,
    tb,
    f1,
    t2,
    f2,
    sens,
    tab,
    rs,
    spread,
    cell,
    mark,
    loc,
    ploc,
    ext,
    row_c,
    lane_a,
    row_a,
    lane_b,
    row_b,
    val_a,
    val_b,
    ret,
    sg,
    psg,
    ys,
    yr,
    ys1,
    yr1,
    zs,
    zr,
    zs1,
    zr1,
    zt,
    sink,
    acc,
    tmat,
    fmat,
    fv,
    oh_lane,
    oh_group,
    row_group,
    column,
    load_sem,
    send_sem,
    recv_sem,
    out_sem,
):
    gx, gy, gz = lax.axis_index("gx"), lax.axis_index("gy"), lax.axis_index("gz")
    zh, c = gz // 2, gz % 2
    even = c == 0
    outer_live = jnp.logical_or(gz == 1, gz == 2)
    partner = (gx, gy, 3 - gz)
    mate = (gx, gy, zh * 2 + (1 - c))
    x_up, x_down = (jnp.minimum(gx + 1, 15), gy, gz), (jnp.maximum(gx - 1, 0), gy, gz)
    has_up, has_down = gx < 15, gx > 0
    first, second = zh == 0, zh == 1
    y_up, y_down = (gx, lax.rem(gy + 1, 4), gz), (gx, lax.rem(gy + 3, 4), gz)
    peers = []
    for j in range(1, 8):
        pgy, pc = lax.rem(gy + j // 2, 4), lax.rem(c + j % 2, 2)
        peers.append((j, pgy, pc, (gx, pgy, zh * 2 + pc)))

    barrier = pltpu.get_barrier_semaphore()

    def greet(device):
        pl.semaphore_signal(barrier, inc=1, device_id=device, device_id_type=MESH)

    pl.when(first)(lambda: greet(partner))
    pl.when(has_up)(lambda: greet(x_up))
    pl.when(has_down)(lambda: greet(x_down))
    for _, _, _, device in peers:
        greet(device)
    expected = 7 + has_up.astype(I32) + has_down.astype(I32) + zh

    loads = {}
    for k, (name, source, target) in enumerate(
        (
            ("t0", t0_hbm, t0p.at[pl.ds(1, NX)]),
            ("dn", dn_hbm, dn),
            ("te", te_hbm, te),
            ("cell", cell_hbm, cell),
            ("mark", cell_hbm, mark),
            ("loc", loc_hbm, loc),
            ("ext", ext_hbm, ext),
            ("coef", coef_hbm, tab.at[gy, c]),
            ("f0", f0_hbm, f0),
            ("st", st_hbm, st),
            ("pe", pe_hbm, pe),
        )
    ):
        loads[name] = pltpu.make_async_copy(source, target, load_sem.at[k])
        loads[name].start()

    sent = []

    def remote(source, target, index, device):
        return pltpu.make_async_remote_copy(
            src_ref=source,
            dst_ref=target,
            send_sem=send_sem.at[index],
            recv_sem=recv_sem.at[index],
            device_id=device,
            device_id_type=MESH,
        )

    def send(source, target, index, device):
        copy = remote(source, target, index, device)
        copy.start()
        sent.append(copy.wait_send)
        return copy

    def send_x(padded, index):
        down = remote(padded.at[1], padded.at[NX + 1], index, x_down)
        up = remote(padded.at[NX], padded.at[0], index + 1, x_up)
        pl.when(has_down)(down.start)
        pl.when(has_up)(up.start)
        sent.append(lambda: pl.when(has_down)(down.wait_send))
        sent.append(lambda: pl.when(has_up)(up.wait_send))

        def arrived():
            pl.when(has_up)(down.wait_recv)
            pl.when(has_down)(up.wait_recv)
            padded[0] = jnp.where(has_down, padded[0], 0.0)
            padded[NX + 1] = jnp.where(has_up, padded[NX + 1], 0.0)

        return arrived

    base = lax.broadcasted_iota(I32, (256, 128), 0).astype(F32).astype(BF16)
    column[...] = base

    loads["t0"].wait()
    loads["dn"].wait()
    loads["te"].wait()

    @pl.loop(0, NX, unroll=2)
    def _(i):
        wp[i + 1] = dn[i] * te[i]

    for k, padded in enumerate((t0p, wp)):
        ys[0, k] = padded[1:17, 0:1, :]
        ys[1, k] = padded[1:17, NY - 1 : NY, :]
        left, right = z_faces(padded[1:17])
        zs[0, k : k + 1] = jnp.where(even, right, left)
        zs[1, k : k + 1] = jnp.where(even, left, right)

    pl.semaphore_wait(barrier, expected)
    table = [send(coef_hbm, tab.at[gy, c], j, device) for j, _, _, device in peers]
    request = remote(loc_hbm, ploc, 0, partner)
    outer = remote(zs.at[1], zr.at[1], 8, partner)

    def ask():
        request.start()
        outer.start()

    pl.when(second)(ask)
    halo = [
        send(zs.at[0], zr.at[0], 9, mate),
        send(ys.at[0], yr.at[1], 14, y_down),
        send(ys.at[1], yr.at[0], 15, y_up),
    ]
    halo_x = [send_x(t0p, 10), send_x(wp, 12)]
    sent.append(request.wait_send)
    sent.append(outer.wait_send)

    for name in ("cell", "loc", "ext"):
        loads[name].wait()
    loads["mark"].wait()
    cell_row = cell[...] >> 8
    oh_lane[...] = one_hot((cell[...] & (NZ - 1)).astype(F32).astype(BF16), column[...], NZ)
    row_c[...] = cell_row
    row, lane = decode(loc[...], gx, zh)
    row_a[...], lane_a[...] = row, lane.astype(F32)
    slot = lax.broadcasted_iota(I32, (1, SLOTS), 1)
    ext[...] = jnp.where(slot < active[0], ext[...], 0.0)
    for name in ("f0", "st", "pe"):
        loads[name].wait()

    visits = []
    group, window = jnp.int32(0), jnp.int32(0)
    for _ in range(VISITS):
        over = group >= GROUPS
        at = jnp.minimum(group, GROUPS - 1)
        visits.append((at, window, jnp.where(over, -1, window * WIDTH)))
        last = mark[0, at * GROUP + (GROUP - 1)] >> 8
        more = jnp.logical_and(last >= (window + 1) * WIDTH, jnp.logical_not(over))
        window = jnp.where(more, window + 1, window)
        group = jnp.where(more, group, group + 1)

    for k in range(GROUPS):
        oh_group[k] = oh_lane[:, k * GROUP : (k + 1) * GROUP]
        row_group[k] = row_c[:, k * GROUP : (k + 1) * GROUP]

    def put(k, i, x):
        high, low = halves(x)
        rows = pl.ds(pl.multiple_of(lax.rem(i, 2) * NY, NY), NY)
        fmat[i // 2, k, rows, 0:NZ] = high
        fmat[i // 2, k, rows, NZ : 2 * NZ] = low

    def pick(fields):
        lo, hi = fields
        count = hi - lo
        found = []
        for at, window, start in visits:
            hot = oh_group[at]
            part = jnp.dot(
                fmat[window, lo:hi].reshape(count * WIDTH, 2 * NZ),
                jnp.concatenate([hot, hot], axis=0),
                preferred_element_type=F32,
            )
            wanted = jnp.where(start < 0, -1, row_group[at] - start)
            hit = row_hit(wanted, WIDTH)
            found.append(
                [
                    jnp.sum(
                        jnp.where(hit, part[f * WIDTH : (f + 1) * WIDTH], 0.0),
                        axis=0,
                        keepdims=True,
                    )
                    for f in range(count)
                ]
            )
        for k in range(GROUPS):
            for f in range(count):
                total = jnp.zeros((1, GROUP), F32)
                for (at, _, _), values in zip(visits, found):
                    total = total + jnp.where(at == k, values[f], 0.0)
                fv[lo + f, :, k * GROUP : (k + 1) * GROUP] = total

    @pl.loop(0, NX, unroll=2)
    def _(i):
        t, tw = t0p[i + 1], te[i]
        lifted = t - bath
        growth = rate(st[i]) * (1.0 - f0[i]) * gate(t)
        new = f0[i] + growth
        f1[i] = new
        tb[i] = enthalpy * growth
        slope = (enthalpy * tw + pe[i]) * (rate(st[i]) * (1.0 - new)) * -sharpness
        put(0, i, lifted)
        put(1, i, tw * lifted)
        put(2, i, slope * lifted)

    def gather(matrix, size, hot, row, out):
        found = jnp.dot(
            matrix[...], jnp.concatenate([hot, hot], axis=0), preferred_element_type=F32
        )
        found = jnp.where(row_hit(row, size), found, 0.0)
        out[...] = jnp.sum(found, axis=0, keepdims=True)

    def scatter(value, size, hot, row):
        high, low = halves(value)
        right = jnp.concatenate(
            [hot * jnp.broadcast_to(high, hot.shape), hot * jnp.broadcast_to(low, hot.shape)],
            axis=1,
        )
        left = jnp.where(row_hit(row, size), 1.0, 0.0).astype(BF16)
        return lax.dot_general(
            jnp.concatenate([left, left], axis=1),
            right,
            (((1,), (1,)), ((), ())),
            preferred_element_type=F32,
        )

    def hot_lanes(ref):
        return one_hot(ref[...].astype(BF16), column[...], 256)

    pick((0, 3))

    loads["coef"].wait()
    for copy in table:
        copy.wait_recv()
    pieces = []
    for part in range(2):
        pieces.append(halves(tab[:, part].reshape(HROWS, 128)))
    tmat[...] = jnp.concatenate(
        [pieces[0][0], pieces[1][0], pieces[0][1], pieces[1][1]], axis=1
    )
    gather(tmat, HROWS, hot_lanes(lane_a), row_a[...], val_a)

    request.wait_recv()
    pl.when(first)(ask)
    row, lane = decode(ploc[...], gx, zh)
    row_b[...], lane_b[...] = row, lane.astype(F32)
    gather(tmat, HROWS, hot_lanes(lane_b), row_b[...], val_b)
    reply = send(val_b, ret, 16, partner)

    for copy in halo:
        copy.wait_recv()
    for arrived in halo_x:
        arrived()
    outer.wait_recv()
    yr[0] = jnp.where(gy > 0, yr[0], 0.0)
    yr[1] = jnp.where(gy < 3, yr[1], 0.0)

    def z_halo(inner, outer):
        outer = jnp.where(outer_live, outer, 0.0)
        return z_block(jnp.where(even, outer, inner), jnp.where(even, inner, outer))

    for k in range(2):
        zt[k] = z_halo(zr[0, k : k + 1], zr[1, k : k + 1])

    @pl.loop(0, NX, unroll=2)
    def _(i):
        t = t0p[i + 1]
        around = neighbours(t, t0p[i], t0p[i + 2], yr[0, 0, i], yr[1, 0, i], zt[0, i])
        adjoint = neighbours(wp[i + 1], wp[i], wp[i + 2], yr[0, 1, i], yr[1, 1, i], zt[1, i])
        d, tw = dn[i], te[i]
        plain = t + d * (around - 6.0 * t) + tb[i]
        tb[i] = plain
        put(3, i, plain)
        put(4, i, tw * (plain - bath) + (tw * (1.0 - 6.0 * d) + adjoint) * (t - bath))

    pick((3, 5))

    reply.wait_recv()
    drain = ext[...] * (val_a[...] + ret[...])
    val_a[...] = drain
    g = gate(fv[3] - drain * fv[0])
    sg[...] = -ext[...] * (fv[4] - 2.0 * drain * fv[1] + fv[2] * (g * (1.0 - g)))
    slots = send(sg, psg, 17, partner)
    sink[...] = scatter(val_a[...], ROWS, oh_lane[...], row_c[...])

    @pl.loop(0, NX, unroll=2)
    def _(i):
        rows = pl.ds(pl.multiple_of(i * NY, NY), NY)
        drain = sink[rows, :]
        t1 = tb[i] - drain * (t0p[i + 1] - bath)
        t1p[i + 1] = t1
        growth = rate(st[i]) * (1.0 - f1[i]) * gate(t1)
        f2[i] = f1[i] + growth
        t2[i] = t1 - 6.0 * dn[i] * t1 + enthalpy * growth - drain * (t1 - bath)

    frac_copy = pltpu.make_async_copy(f2, frac_out, out_sem.at[0])
    frac_copy.start()
    ys1[0] = t1p[1:17, 0:1, :]
    ys1[1] = t1p[1:17, NY - 1 : NY, :]
    left, right = z_faces(t1p[1:17])
    zs1[0] = jnp.where(even, right, left)
    zs1[1] = jnp.where(even, left, right)
    halo = [
        send(zs1.at[1], zr1.at[1], 18, partner),
        send(zs1.at[0], zr1.at[0], 19, mate),
        send(ys1.at[0], yr1.at[1], 22, y_down),
        send(ys1.at[1], yr1.at[0], 23, y_up),
    ]
    halo_x = send_x(t1p, 20)
    acc[...] = scatter(sg[...], HROWS, hot_lanes(lane_a), row_a[...])
    slots.wait_recv()
    acc[...] += scatter(psg[...], HROWS, hot_lanes(lane_b), row_b[...])
    for g in range(4):
        for part in range(2):
            spread[g, part] = acc[g * CROWS : (g + 1) * CROWS, part * 128 : (part + 1) * 128]
    shares = [
        send(spread.at[pgy, pc], rs.at[j], 23 + j, device) for j, pgy, pc, device in peers
    ]

    for copy in halo:
        copy.wait_recv()
    halo_x()
    yr1[0] = jnp.where(gy > 0, yr1[0], 0.0)
    yr1[1] = jnp.where(gy < 3, yr1[1], 0.0)
    zt[0] = z_halo(zr1[0], zr1[1])

    @pl.loop(0, NX, unroll=4)
    def _(i):
        around = neighbours(
            t1p[i + 1], t1p[i], t1p[i + 2], yr1[0, i], yr1[1, i], zt[0, i]
        )
        t2[i] = t2[i] + dn[i] * around

    temp_copy = pltpu.make_async_copy(t2, temp_out, out_sem.at[1])
    temp_copy.start()
    total = spread[gy, c]
    for copy, (j, _, _, _) in zip(shares, peers):
        copy.wait_recv()
        total = total + rs[j]
    sens[...] = total
    sens_copy = pltpu.make_async_copy(sens, sens_out, out_sem.at[2])
    sens_copy.start()
    for wait in sent:
        wait()
    frac_copy.wait()
    temp_copy.wait()
    sens_copy.wait()


def deliver(t2, f2, sens, temp_out, frac_out, sens_out, t2v, f2v, sv, read_sem, write_sem):
    pieces = []
    for source, middle, target in ((t2, t2v, temp_out), (f2, f2v, frac_out)):
        for k in range(4):
            part = pl.ds(4 * k, 4)
            pieces.append((source.at[part], middle.at[part], target.at[part]))
    pieces.append((sens, sv, sens_out))
    reads = [
        pltpu.make_async_copy(a, b, read_sem.at[k]) for k, (a, b, _) in enumerate(pieces)
    ]
    writes = [
        pltpu.make_async_copy(b, c, write_sem.at[k]) for k, (_, b, c) in enumerate(pieces)
    ]
    for read in reads:
        read.start()
    for read, write in zip(reads, writes):
        read.wait()
        write.start()
    for write in writes:
        write.wait()


def on_device(t0, f0, dn, st, coef, cell, loc, ext, active, te, pe):
    field = (NX, NY, NZ)
    padded = (NX + 2, NY, NZ)
    row = (1, SLOTS)
    vmem = pltpu.VMEM
    anywhere = pl.BlockSpec(memory_space=pl.ANY)
    scratch = (
        [vmem(padded, F32)] * 3
        + [vmem(field, F32)] * 2
        + [vmem(field, I32)]
        + [vmem(field, F32)] * 6
        + [vmem((CROWS, 128), F32)]
        + [
            vmem((4, 2, CROWS, 128), F32),
            vmem((8, CROWS, 128), F32),
            vmem((4, 2, CROWS, 128), F32),
            vmem(row, I32),
            pltpu.SMEM(row, I32),
            vmem(row, I32),
            vmem(row, I32),
            vmem(row, F32),
        ]
        + [vmem(row, I32)]
        + [vmem(row, F32), vmem(row, I32)] * 2
        + [vmem(row, F32)] * 5
        + [vmem((2, 2, NX, 1, NZ), F32)] * 2
        + [vmem((2, NX, 1, NZ), F32)] * 2
        + [vmem((2, 2, ROWS), F32)] * 2
        + [vmem((2, 1, ROWS), F32)] * 2
        + [
            vmem((2, NX, NY, 128), F32),
            vmem((ROWS, NZ), F32),
            vmem((HROWS, 256), F32),
            vmem((HROWS, 512), BF16),
            vmem((WINDOWS, 5, WIDTH, 512), BF16),
            vmem((5, 1, SLOTS), F32),
            vmem((NZ, SLOTS), BF16),
            vmem((GROUPS, NZ, GROUP), BF16),
            vmem((GROUPS, 1, GROUP), I32),
            vmem((256, 128), BF16),
            pltpu.SemaphoreType.DMA((11,)),
            pltpu.SemaphoreType.DMA((31,)),
            pltpu.SemaphoreType.DMA((31,)),
            pltpu.SemaphoreType.DMA((3,)),
        ]
    )
    results = (
        jax.ShapeDtypeStruct(field, F32),
        jax.ShapeDtypeStruct(field, F32),
        jax.ShapeDtypeStruct((CROWS, 128), F32),
    )
    done = pl.pallas_call(
        kernel,
        out_shape=results,
        in_specs=[pl.BlockSpec(memory_space=pltpu.SMEM)] + [anywhere] * 10,
        out_specs=(anywhere,) * 3,
        scratch_shapes=scratch,
        compiler_params=pltpu.CompilerParams(
            collective_id=0, has_side_effects=True, vmem_limit_bytes=56 * 2**20
        ),
    )(
        active,
        t0,
        f0,
        dn,
        st,
        coef.reshape(CROWS, 128),
        cell.reshape(row),
        loc.reshape(row),
        ext.reshape(row),
        te,
        pe,
    )
    temp, frac, sens = pl.pallas_call(
        deliver,
        out_shape=results,
        in_specs=[anywhere] * 3,
        out_specs=(anywhere,) * 3,
        scratch_shapes=[vmem(field, F32)] * 2
        + [vmem((CROWS, 128), F32)]
        + [pltpu.SemaphoreType.DMA((9,))] * 2,
    )(*done)
    return temp, frac, sens.reshape(CHUNK)


def solution(mesh):
    brick, line = P("gx", "gy", "gz"), P(("gx", "gy", "gz"))
    return jax.shard_map(
        on_device,
        mesh=mesh,
        in_specs=(brick,) * 4 + (line,) * 5 + (brick,) * 2,
        out_specs=(brick, brick, line),
        check_vma=False,
    )
```

```python
import functools

import jax
import jax.numpy as jnp
from jax import lax
from jax.experimental import pallas as pl
from jax.experimental.pallas import tpu as pltpu
from jax.sharding import PartitionSpec as P

MESH = pl.DeviceIdType.MESH
F32 = jnp.float32
BF16 = jnp.bfloat16
I32 = jnp.int32

NX, NY, NZ = 16, 32, 256
ROWS = NX * NY
SLOTS = 2048
CHUNK = 7168
CROWS = CHUNK // 128
HROWS = 4 * CROWS
SLAB = 16 * CHUNK
GROUP = 256
GROUPS = SLOTS // GROUP
WIDTH = 64
WINDOWS = ROWS // WIDTH
VISITS = GROUPS + WINDOWS - 1

sharpness = 4.0
kinetic_fast = 0.6
kinetic_slow = 0.2
enthalpy = 0.4
bath = -2.0


def halves(x):
    high = x.astype(BF16)
    return high, (x - high.astype(F32)).astype(BF16)


def one_hot(index, column, size):
    column = jnp.concatenate([column] * (index.shape[1] // 128), axis=1)
    hit = column == jnp.broadcast_to(index, (size, index.shape[1]))
    return jnp.where(hit, jnp.ones((), BF16), jnp.zeros((), BF16))


def row_hit(index, size):
    rows = lax.broadcasted_iota(I32, (size, index.shape[1]), 0)
    return rows == index


def gate(t):
    return jax.nn.sigmoid(sharpness * (0.0 - t))


def rate(status):
    return jnp.where(status == 1, kinetic_fast, jnp.where(status == 2, kinetic_slow, 0.0))


def decode(loc, gx, zh):
    local = loc - gx * SLAB
    row = local >> 7
    owner = (row * 1171) >> 16
    inner = row - owner * CROWS
    mine = ((owner >> 1) & 1) == zh
    return jnp.where(mine, (owner >> 2) * CROWS + inner, -1), (owner & 1) * 128 + (local & 127)


def neighbours(center, low, high, y_low, y_high, z_edge):
    y = lax.broadcasted_iota(I32, (NY, NZ), 0)
    z = lax.broadcasted_iota(I32, (NY, NZ), 1)
    edge = jnp.concatenate([z_edge, z_edge], axis=1)
    total = low + high
    total = total + jnp.where(y == 0, y_low, pltpu.roll(center, 1, 0))
    total = total + jnp.where(y == NY - 1, y_high, pltpu.roll(center, NY - 1, 0))
    total = total + jnp.where(z == 0, edge, pltpu.roll(center, 1, 1))
    return total + jnp.where(z == NZ - 1, edge, pltpu.roll(center, NZ - 1, 1))


def z_faces(x):
    x = x.reshape(ROWS, NZ)
    lane = lax.broadcasted_iota(I32, (ROWS, 128), 1)
    both = jnp.where(lane == 0, x[:, :128], x[:, 128:]).T
    return both[0:1, :], both[127:128, :]


def z_block(left, right):
    row = lax.broadcasted_iota(I32, (128, ROWS), 0)
    both = jnp.where(row == 0, left, jnp.where(row == 127, right, 0.0))
    return both.T.reshape(NX, NY, 128)


def kernel(
    active,
    t0_hbm,
    f0_hbm,
    dn_hbm,
    st_hbm,
    coef_hbm,
    cell_hbm,
    loc_hbm,
    ext_hbm,
    te_hbm,
    pe_hbm,
    temp_out,
    frac_out,
    sens_out,
    t0p,
    wp,
    t1p,
    f0,
    dn,
    st,
    te,
    pe,
    tb,
    f1,
    t2,
    f2,
    sens,
    tab,
    rs,
    spread,
    cell,
    mark,
    loc,
    ploc,
    ext,
    row_c,
    lane_a,
    row_a,
    lane_b,
    row_b,
    val_a,
    val_b,
    ret,
    sg,
    psg,
    ys,
    yr,
    ys1,
    yr1,
    zs,
    zr,
    zs1,
    zr1,
    zt,
    sink,
    acc,
    tmat,
    fmat,
    fv,
    pfv,
    oh_lane,
    oh_group,
    row_group,
    column,
    load_sem,
    send_sem,
    recv_sem,
    out_sem,
):
    gx, gy, gz = lax.axis_index("gx"), lax.axis_index("gy"), lax.axis_index("gz")
    zh, c = gz // 2, gz % 2
    even = c == 0
    outer_live = jnp.logical_or(gz == 1, gz == 2)
    partner = (gx, gy, 3 - gz)
    mate = (gx, gy, zh * 2 + (1 - c))
    x_up, x_down = (jnp.minimum(gx + 1, 15), gy, gz), (jnp.maximum(gx - 1, 0), gy, gz)
    has_up, has_down = gx < 15, gx > 0
    y_up, y_down = (gx, lax.rem(gy + 1, 4), gz), (gx, lax.rem(gy + 3, 4), gz)
    peers = []
    for j in range(1, 8):
        pgy, pc = lax.rem(gy + j // 2, 4), lax.rem(c + j % 2, 2)
        peers.append((j, pgy, pc, (gx, pgy, zh * 2 + pc)))

    barrier = pltpu.get_barrier_semaphore()

    def greet(device):
        pl.semaphore_signal(barrier, inc=1, device_id=device, device_id_type=MESH)

    greet(partner)
    pl.when(has_up)(lambda: greet(x_up))
    pl.when(has_down)(lambda: greet(x_down))
    for _, _, _, device in peers:
        greet(device)
    expected = 7 + has_up.astype(I32) + has_down.astype(I32) + 1

    loads = {}
    for k, (name, source, target) in enumerate(
        (
            ("t0", t0_hbm, t0p.at[pl.ds(1, NX)]),
            ("dn", dn_hbm, dn),
            ("te", te_hbm, te),
            ("cell", cell_hbm, cell),
            ("mark", cell_hbm, mark),
            ("loc", loc_hbm, loc),
            ("ext", ext_hbm, ext),
            ("coef", coef_hbm, tab.at[gy, c]),
            ("f0", f0_hbm, f0),
            ("st", st_hbm, st),
            ("pe", pe_hbm, pe),
        )
    ):
        loads[name] = pltpu.make_async_copy(source, target, load_sem.at[k])
        loads[name].start()

    sent = []

    def remote(source, target, index, device):
        return pltpu.make_async_remote_copy(
            src_ref=source,
            dst_ref=target,
            send_sem=send_sem.at[index],
            recv_sem=recv_sem.at[index],
            device_id=device,
            device_id_type=MESH,
        )

    def send(source, target, index, device):
        copy = remote(source, target, index, device)
        copy.start()
        sent.append(copy.wait_send)
        return copy

    def send_x(padded, index):
        down = remote(padded.at[1], padded.at[NX + 1], index, x_down)
        up = remote(padded.at[NX], padded.at[0], index + 1, x_up)
        pl.when(has_down)(down.start)
        pl.when(has_up)(up.start)
        sent.append(lambda: pl.when(has_down)(down.wait_send))
        sent.append(lambda: pl.when(has_up)(up.wait_send))

        def arrived():
            pl.when(has_up)(down.wait_recv)
            pl.when(has_down)(up.wait_recv)
            padded[0] = jnp.where(has_down, padded[0], 0.0)
            padded[NX + 1] = jnp.where(has_up, padded[NX + 1], 0.0)

        return arrived

    base = lax.broadcasted_iota(I32, (256, 128), 0).astype(F32).astype(BF16)
    column[...] = base

    loads["t0"].wait()
    loads["dn"].wait()
    loads["te"].wait()

    @pl.loop(0, NX, unroll=2)
    def _(i):
        wp[i + 1] = dn[i] * te[i]

    for k, padded in enumerate((t0p, wp)):
        ys[0, k] = padded[1:17, 0:1, :]
        ys[1, k] = padded[1:17, NY - 1 : NY, :]
        left, right = z_faces(padded[1:17])
        zs[0, k : k + 1] = jnp.where(even, right, left)
        zs[1, k : k + 1] = jnp.where(even, left, right)

    pl.semaphore_wait(barrier, expected)
    request = send(loc_hbm, ploc, 0, partner)
    outer = send(zs.at[1], zr.at[1], 8, partner)
    table = [send(coef_hbm, tab.at[gy, c], j, device) for j, _, _, device in peers]
    halo = [
        send(zs.at[0], zr.at[0], 9, mate),
        send(ys.at[0], yr.at[1], 14, y_down),
        send(ys.at[1], yr.at[0], 15, y_up),
    ]
    halo_x = [send_x(t0p, 10), send_x(wp, 12)]

    for name in ("cell", "loc", "ext"):
        loads[name].wait()
    loads["mark"].wait()
    cell_row = cell[...] >> 8
    oh_lane[...] = one_hot((cell[...] & (NZ - 1)).astype(F32).astype(BF16), column[...], NZ)
    row_c[...] = cell_row
    row, lane = decode(loc[...], gx, zh)
    row_a[...], lane_a[...] = row, lane.astype(F32)
    slot = lax.broadcasted_iota(I32, (1, SLOTS), 1)
    ext[...] = jnp.where(slot < active[0], ext[...], 0.0)
    for name in ("f0", "st", "pe"):
        loads[name].wait()

    visits = []
    group, window = jnp.int32(0), jnp.int32(0)
    for _ in range(VISITS):
        over = group >= GROUPS
        at = jnp.minimum(group, GROUPS - 1)
        visits.append((at, window, jnp.where(over, -1, window * WIDTH)))
        last = mark[0, at * GROUP + (GROUP - 1)] >> 8
        more = jnp.logical_and(last >= (window + 1) * WIDTH, jnp.logical_not(over))
        window = jnp.where(more, window + 1, window)
        group = jnp.where(more, group, group + 1)

    for k in range(GROUPS):
        oh_group[k] = oh_lane[:, k * GROUP : (k + 1) * GROUP]
        row_group[k] = row_c[:, k * GROUP : (k + 1) * GROUP]

    def put(k, i, x):
        high, low = halves(x)
        rows = pl.ds(pl.multiple_of(lax.rem(i, 2) * NY, NY), NY)
        fmat[i // 2, k, rows, 0:NZ] = high
        fmat[i // 2, k, rows, NZ : 2 * NZ] = low

    def pick(fields):
        lo, hi = fields
        count = hi - lo
        found = []
        for at, window, start in visits:
            hot = oh_group[at]
            part = jnp.dot(
                fmat[window, lo:hi].reshape(count * WIDTH, 2 * NZ),
                jnp.concatenate([hot, hot], axis=0),
                preferred_element_type=F32,
            )
            wanted = jnp.where(start < 0, -1, row_group[at] - start)
            hit = row_hit(wanted, WIDTH)
            found.append(
                [
                    jnp.sum(
                        jnp.where(hit, part[f * WIDTH : (f + 1) * WIDTH], 0.0),
                        axis=0,
                        keepdims=True,
                    )
                    for f in range(count)
                ]
            )
        for k in range(GROUPS):
            for f in range(count):
                total = jnp.zeros((1, GROUP), F32)
                for (at, _, _), values in zip(visits, found):
                    total = total + jnp.where(at == k, values[f], 0.0)
                fv[lo + f, :, k * GROUP : (k + 1) * GROUP] = total

    @pl.loop(0, NX, unroll=2)
    def _(i):
        t, tw = t0p[i + 1], te[i]
        lifted = t - bath
        growth = rate(st[i]) * (1.0 - f0[i]) * gate(t)
        new = f0[i] + growth
        f1[i] = new
        tb[i] = enthalpy * growth
        slope = (enthalpy * tw + pe[i]) * (rate(st[i]) * (1.0 - new)) * -sharpness
        put(0, i, lifted)
        put(1, i, tw * lifted)
        put(2, i, slope * lifted)

    def gather(matrix, size, hot, row, out):
        found = jnp.dot(
            matrix[...], jnp.concatenate([hot, hot], axis=0), preferred_element_type=F32
        )
        found = jnp.where(row_hit(row, size), found, 0.0)
        out[...] = jnp.sum(found, axis=0, keepdims=True)

    def scatter(value, size, hot, row):
        high, low = halves(value)
        right = jnp.concatenate(
            [hot * jnp.broadcast_to(high, hot.shape), hot * jnp.broadcast_to(low, hot.shape)],
            axis=1,
        )
        left = jnp.where(row_hit(row, size), 1.0, 0.0).astype(BF16)
        return lax.dot_general(
            jnp.concatenate([left, left], axis=1),
            right,
            (((1,), (1,)), ((), ())),
            preferred_element_type=F32,
        )

    def hot_lanes(ref):
        return one_hot(ref[...].astype(BF16), column[...], 256)

    pick((0, 3))
    fv[0] = ext[...] * fv[0]
    fv[1] = ext[...] * (ext[...] * fv[1])
    fv[2] = ext[...] * fv[2]
    early = send(fv.at[pl.ds(0, 3)], pfv.at[pl.ds(0, 3)], 17, partner)

    def slot_gradient(value, kept):
        g = gate(kept[3] - value * kept[0])
        return 2.0 * value * kept[1] - kept[4] - kept[2] * (g * (1.0 - g))


    loads["coef"].wait()
    for copy in table:
        copy.wait_recv()
    pieces = []
    for part in range(2):
        pieces.append(halves(tab[:, part].reshape(HROWS, 128)))
    tmat[...] = jnp.concatenate(
        [pieces[0][0], pieces[1][0], pieces[0][1], pieces[1][1]], axis=1
    )

    request.wait_recv()
    row, lane = decode(ploc[...], gx, zh)
    row_b[...], lane_b[...] = row, lane.astype(F32)
    gather(tmat, HROWS, hot_lanes(lane_b), row_b[...], val_b)
    reply = send(val_b, ret, 16, partner)

    for copy in halo:
        copy.wait_recv()
    for arrived in halo_x:
        arrived()
    outer.wait_recv()
    yr[0] = jnp.where(gy > 0, yr[0], 0.0)
    yr[1] = jnp.where(gy < 3, yr[1], 0.0)

    def z_halo(inner, outer):
        outer = jnp.where(outer_live, outer, 0.0)
        return z_block(jnp.where(even, outer, inner), jnp.where(even, inner, outer))

    for k in range(2):
        zt[k] = z_halo(zr[0, k : k + 1], zr[1, k : k + 1])

    @pl.loop(0, NX, unroll=2)
    def _(i):
        t = t0p[i + 1]
        around = neighbours(t, t0p[i], t0p[i + 2], yr[0, 0, i], yr[1, 0, i], zt[0, i])
        adjoint = neighbours(wp[i + 1], wp[i], wp[i + 2], yr[0, 1, i], yr[1, 1, i], zt[1, i])
        d, tw = dn[i], te[i]
        plain = t + d * (around - 6.0 * t) + tb[i]
        tb[i] = plain
        put(3, i, plain)
        put(4, i, tw * (plain - bath) + (tw * (1.0 - 6.0 * d) + adjoint) * (t - bath))

    pick((3, 5))
    fv[4] = ext[...] * fv[4]
    late = send(fv.at[pl.ds(3, 2)], pfv.at[pl.ds(3, 2)], 31, partner)
    gather(tmat, HROWS, hot_lanes(lane_a), row_a[...], val_a)

    sg[...] = slot_gradient(val_a[...], fv)
    acc[...] = scatter(sg[...], HROWS, hot_lanes(lane_a), row_a[...])

    reply.wait_recv()
    val_a[...] = ext[...] * (val_a[...] + ret[...])
    sink[...] = scatter(val_a[...], ROWS, oh_lane[...], row_c[...])

    @pl.loop(0, NX, unroll=4)
    def _(i):
        rows = pl.ds(pl.multiple_of(i * NY, NY), NY)
        t1p[i + 1] = tb[i] - sink[rows, :] * (t0p[i + 1] - bath)

    ys1[0] = t1p[1:17, 0:1, :]
    ys1[1] = t1p[1:17, NY - 1 : NY, :]
    left, right = z_faces(t1p[1:17])
    zs1[0] = jnp.where(even, right, left)
    zs1[1] = jnp.where(even, left, right)
    halo = [
        send(zs1.at[1], zr1.at[1], 18, partner),
        send(zs1.at[0], zr1.at[0], 19, mate),
        send(ys1.at[0], yr1.at[1], 22, y_down),
        send(ys1.at[1], yr1.at[0], 23, y_up),
    ]
    halo_x = send_x(t1p, 20)
    early.wait_recv()
    late.wait_recv()
    psg[...] = slot_gradient(val_b[...], pfv)
    acc[...] += scatter(psg[...], HROWS, hot_lanes(lane_b), row_b[...])
    for g in range(4):
        for part in range(2):
            spread[g, part] = acc[g * CROWS : (g + 1) * CROWS, part * 128 : (part + 1) * 128]
    shares = [
        send(spread.at[pgy, pc], rs.at[j], 23 + j, device) for j, pgy, pc, device in peers
    ]

    @pl.loop(0, NX, unroll=2)
    def _(i):
        rows = pl.ds(pl.multiple_of(i * NY, NY), NY)
        drain = sink[rows, :]
        t1 = t1p[i + 1]
        growth = rate(st[i]) * (1.0 - f1[i]) * gate(t1)
        f2[i] = f1[i] + growth
        t2[i] = t1 - 6.0 * dn[i] * t1 + enthalpy * growth - drain * (t1 - bath)

    frac_copy = pltpu.make_async_copy(f2, frac_out, out_sem.at[0])
    frac_copy.start()
    for copy in halo:
        copy.wait_recv()
    halo_x()
    yr1[0] = jnp.where(gy > 0, yr1[0], 0.0)
    yr1[1] = jnp.where(gy < 3, yr1[1], 0.0)
    zt[0] = z_halo(zr1[0], zr1[1])

    @pl.loop(0, NX, unroll=4)
    def _(i):
        around = neighbours(
            t1p[i + 1], t1p[i], t1p[i + 2], yr1[0, i], yr1[1, i], zt[0, i]
        )
        t2[i] = t2[i] + dn[i] * around

    temp_copy = pltpu.make_async_copy(t2, temp_out, out_sem.at[1])
    temp_copy.start()
    total = spread[gy, c]
    for copy, (j, _, _, _) in zip(shares, peers):
        copy.wait_recv()
        total = total + rs[j]
    sens[...] = total
    sens_copy = pltpu.make_async_copy(sens, sens_out, out_sem.at[2])
    sens_copy.start()
    for wait in sent:
        wait()
    frac_copy.wait()
    temp_copy.wait()
    sens_copy.wait()


def deliver(t2, f2, sens, temp_out, frac_out, sens_out, t2v, f2v, sv, read_sem, write_sem):
    pieces = []
    for source, middle, target in ((t2, t2v, temp_out), (f2, f2v, frac_out)):
        for k in range(4):
            part = pl.ds(4 * k, 4)
            pieces.append((source.at[part], middle.at[part], target.at[part]))
    pieces.append((sens, sv, sens_out))
    reads = [
        pltpu.make_async_copy(a, b, read_sem.at[k]) for k, (a, b, _) in enumerate(pieces)
    ]
    writes = [
        pltpu.make_async_copy(b, c, write_sem.at[k]) for k, (_, b, c) in enumerate(pieces)
    ]
    for read in reads:
        read.start()
    for read, write in zip(reads, writes):
        read.wait()
        write.start()
    for write in writes:
        write.wait()


def on_device(t0, f0, dn, st, coef, cell, loc, ext, active, te, pe):
    field = (NX, NY, NZ)
    padded = (NX + 2, NY, NZ)
    row = (1, SLOTS)
    vmem = pltpu.VMEM
    anywhere = pl.BlockSpec(memory_space=pl.ANY)
    scratch = (
        [vmem(padded, F32)] * 3
        + [vmem(field, F32)] * 2
        + [vmem(field, I32)]
        + [vmem(field, F32)] * 6
        + [vmem((CROWS, 128), F32)]
        + [
            vmem((4, 2, CROWS, 128), F32),
            vmem((8, CROWS, 128), F32),
            vmem((4, 2, CROWS, 128), F32),
            vmem(row, I32),
            pltpu.SMEM(row, I32),
            vmem(row, I32),
            vmem(row, I32),
            vmem(row, F32),
        ]
        + [vmem(row, I32)]
        + [vmem(row, F32), vmem(row, I32)] * 2
        + [vmem(row, F32)] * 5
        + [vmem((2, 2, NX, 1, NZ), F32)] * 2
        + [vmem((2, NX, 1, NZ), F32)] * 2
        + [vmem((2, 2, ROWS), F32)] * 2
        + [vmem((2, 1, ROWS), F32)] * 2
        + [
            vmem((2, NX, NY, 128), F32),
            vmem((ROWS, NZ), F32),
            vmem((HROWS, 256), F32),
            vmem((HROWS, 512), BF16),
            vmem((WINDOWS, 5, WIDTH, 512), BF16),
            vmem((5, 1, SLOTS), F32),
            vmem((5, 1, SLOTS), F32),
            vmem((NZ, SLOTS), BF16),
            vmem((GROUPS, NZ, GROUP), BF16),
            vmem((GROUPS, 1, GROUP), I32),
            vmem((256, 128), BF16),
            pltpu.SemaphoreType.DMA((11,)),
            pltpu.SemaphoreType.DMA((32,)),
            pltpu.SemaphoreType.DMA((32,)),
            pltpu.SemaphoreType.DMA((3,)),
        ]
    )
    results = (
        jax.ShapeDtypeStruct(field, F32),
        jax.ShapeDtypeStruct(field, F32),
        jax.ShapeDtypeStruct((CROWS, 128), F32),
    )
    done = pl.pallas_call(
        kernel,
        out_shape=results,
        in_specs=[pl.BlockSpec(memory_space=pltpu.SMEM)] + [anywhere] * 10,
        out_specs=(anywhere,) * 3,
        scratch_shapes=scratch,
        compiler_params=pltpu.CompilerParams(
            collective_id=0, has_side_effects=True, vmem_limit_bytes=56 * 2**20
        ),
    )(
        active,
        t0,
        f0,
        dn,
        st,
        coef.reshape(CROWS, 128),
        cell.reshape(row),
        loc.reshape(row),
        ext.reshape(row),
        te,
        pe,
    )
    temp, frac, sens = pl.pallas_call(
        deliver,
        out_shape=results,
        in_specs=[anywhere] * 3,
        out_specs=(anywhere,) * 3,
        scratch_shapes=[vmem(field, F32)] * 2
        + [vmem((CROWS, 128), F32)]
        + [pltpu.SemaphoreType.DMA((9,))] * 2,
    )(*done)
    return temp, frac, sens.reshape(CHUNK)


def solution(mesh):
    brick, line = P("gx", "gy", "gz"), P(("gx", "gy", "gz"))
    return jax.shard_map(
        on_device,
        mesh=mesh,
        in_specs=(brick,) * 4 + (line,) * 5 + (brick,) * 2,
        out_specs=(brick, brick, line),
        check_vma=False,
    )
```

```python
import functools

import jax
import jax.numpy as jnp
from jax import lax
from jax.experimental import pallas as pl
from jax.experimental.pallas import tpu as pltpu
from jax.sharding import PartitionSpec as P

MESH = pl.DeviceIdType.MESH
F32 = jnp.float32
BF16 = jnp.bfloat16
I32 = jnp.int32

NX, NY, NZ = 16, 32, 256
ROWS = NX * NY
SLOTS = 2048
CHUNK = 7168
CROWS = CHUNK // 128
HROWS = 4 * CROWS
SLAB = 16 * CHUNK
GROUP = 256
GROUPS = SLOTS // GROUP
WIDTH = 64
WINDOWS = ROWS // WIDTH
VISITS = GROUPS + WINDOWS - 1

sharpness = 4.0
kinetic_fast = 0.6
kinetic_slow = 0.2
enthalpy = 0.4
bath = -2.0


def halves(x):
    high = x.astype(BF16)
    return high, (x - high.astype(F32)).astype(BF16)


def one_hot(index, column, size):
    column = jnp.concatenate([column] * (index.shape[1] // 128), axis=1)
    hit = column == jnp.broadcast_to(index, (size, index.shape[1]))
    return jnp.where(hit, jnp.ones((), BF16), jnp.zeros((), BF16))


def row_hit(index, size):
    rows = lax.broadcasted_iota(I32, (size, index.shape[1]), 0)
    return rows == index


def gate(t):
    return jax.nn.sigmoid(sharpness * (0.0 - t))


def rate(status):
    return jnp.where(status == 1, kinetic_fast, jnp.where(status == 2, kinetic_slow, 0.0))


def decode(loc, gx, zh):
    local = loc - gx * SLAB
    row = local >> 7
    owner = (row * 1171) >> 16
    inner = row - owner * CROWS
    mine = ((owner >> 1) & 1) == zh
    return jnp.where(mine, (owner >> 2) * CROWS + inner, -1), (owner & 1) * 128 + (local & 127)


def neighbours(center, low, high, y_low, y_high, z_edge):
    y = lax.broadcasted_iota(I32, (NY, NZ), 0)
    z = lax.broadcasted_iota(I32, (NY, NZ), 1)
    edge = jnp.concatenate([z_edge, z_edge], axis=1)
    total = low + high
    total = total + jnp.where(y == 0, y_low, pltpu.roll(center, 1, 0))
    total = total + jnp.where(y == NY - 1, y_high, pltpu.roll(center, NY - 1, 0))
    total = total + jnp.where(z == 0, edge, pltpu.roll(center, 1, 1))
    return total + jnp.where(z == NZ - 1, edge, pltpu.roll(center, NZ - 1, 1))


def z_faces(x):
    x = x.reshape(ROWS, NZ)
    lane = lax.broadcasted_iota(I32, (ROWS, 128), 1)
    both = jnp.where(lane == 0, x[:, :128], x[:, 128:]).T
    return both[0:1, :], both[127:128, :]


def z_block(left, right):
    row = lax.broadcasted_iota(I32, (128, ROWS), 0)
    both = jnp.where(row == 0, left, jnp.where(row == 127, right, 0.0))
    return both.T.reshape(NX, NY, 128)


def kernel(
    active,
    t0_hbm,
    f0_hbm,
    dn_hbm,
    st_hbm,
    coef_hbm,
    cell_hbm,
    loc_hbm,
    ext_hbm,
    te_hbm,
    pe_hbm,
    t2,
    f2,
    sens,
    t0p,
    wp,
    t1p,
    f0,
    dn,
    st,
    te,
    pe,
    tb,
    f1,
    tab,
    rs,
    spread,
    cell,
    mark,
    loc,
    ploc,
    ext,
    row_c,
    lane_a,
    row_a,
    lane_b,
    row_b,
    val_a,
    val_b,
    ret,
    sg,
    psg,
    ys,
    yr,
    ys1,
    yr1,
    zs,
    zr,
    zs1,
    zr1,
    zt,
    sink,
    acc,
    tmat,
    fmat,
    fv,
    pfv,
    oh_lane,
    oh_group,
    row_group,
    column,
    load_sem,
    send_sem,
    recv_sem,
):
    gx, gy, gz = lax.axis_index("gx"), lax.axis_index("gy"), lax.axis_index("gz")
    zh, c = gz // 2, gz % 2
    even = c == 0
    outer_live = jnp.logical_or(gz == 1, gz == 2)
    partner = (gx, gy, 3 - gz)
    mate = (gx, gy, zh * 2 + (1 - c))
    x_up, x_down = (jnp.minimum(gx + 1, 15), gy, gz), (jnp.maximum(gx - 1, 0), gy, gz)
    has_up, has_down = gx < 15, gx > 0
    y_up, y_down = (gx, lax.rem(gy + 1, 4), gz), (gx, lax.rem(gy + 3, 4), gz)
    peers = []
    for j in range(1, 8):
        pgy, pc = lax.rem(gy + j // 2, 4), lax.rem(c + j % 2, 2)
        peers.append((j, pgy, pc, (gx, pgy, zh * 2 + pc)))

    barrier = pltpu.get_barrier_semaphore()

    def greet(device):
        pl.semaphore_signal(barrier, inc=1, device_id=device, device_id_type=MESH)

    greet(partner)
    pl.when(has_up)(lambda: greet(x_up))
    pl.when(has_down)(lambda: greet(x_down))
    for _, _, _, device in peers:
        greet(device)
    expected = 7 + has_up.astype(I32) + has_down.astype(I32) + 1

    loads = {}
    for k, (name, source, target) in enumerate(
        (
            ("t0", t0_hbm, t0p.at[pl.ds(1, NX)]),
            ("dn", dn_hbm, dn),
            ("te", te_hbm, te),
            ("cell", cell_hbm, cell),
            ("mark", cell_hbm, mark),
            ("loc", loc_hbm, loc),
            ("ext", ext_hbm, ext),
            ("coef", coef_hbm, tab.at[gy, c]),
            ("f0", f0_hbm, f0),
            ("st", st_hbm, st),
            ("pe", pe_hbm, pe),
        )
    ):
        loads[name] = pltpu.make_async_copy(source, target, load_sem.at[k])
        loads[name].start()

    sent = []

    def remote(source, target, index, device):
        return pltpu.make_async_remote_copy(
            src_ref=source,
            dst_ref=target,
            send_sem=send_sem.at[index],
            recv_sem=recv_sem.at[index],
            device_id=device,
            device_id_type=MESH,
        )

    def send(source, target, index, device):
        copy = remote(source, target, index, device)
        copy.start()
        sent.append(copy.wait_send)
        return copy

    def send_x(padded, index):
        down = remote(padded.at[1], padded.at[NX + 1], index, x_down)
        up = remote(padded.at[NX], padded.at[0], index + 1, x_up)
        pl.when(has_down)(down.start)
        pl.when(has_up)(up.start)
        sent.append(lambda: pl.when(has_down)(down.wait_send))
        sent.append(lambda: pl.when(has_up)(up.wait_send))

        def arrived():
            pl.when(has_up)(down.wait_recv)
            pl.when(has_down)(up.wait_recv)
            padded[0] = jnp.where(has_down, padded[0], 0.0)
            padded[NX + 1] = jnp.where(has_up, padded[NX + 1], 0.0)

        return arrived

    base = lax.broadcasted_iota(I32, (256, 128), 0).astype(F32).astype(BF16)
    column[...] = base

    loads["t0"].wait()
    loads["dn"].wait()
    loads["te"].wait()

    @pl.loop(0, NX, unroll=2)
    def _(i):
        wp[i + 1] = dn[i] * te[i]

    for k, padded in enumerate((t0p, wp)):
        ys[0, k] = padded[1:17, 0:1, :]
        ys[1, k] = padded[1:17, NY - 1 : NY, :]
        left, right = z_faces(padded[1:17])
        zs[0, k : k + 1] = jnp.where(even, right, left)
        zs[1, k : k + 1] = jnp.where(even, left, right)

    pl.semaphore_wait(barrier, expected)
    request = send(loc_hbm, ploc, 0, partner)
    outer = send(zs.at[1], zr.at[1], 8, partner)
    table = [send(coef_hbm, tab.at[gy, c], j, device) for j, _, _, device in peers]
    halo = [
        send(zs.at[0], zr.at[0], 9, mate),
        send(ys.at[0], yr.at[1], 14, y_down),
        send(ys.at[1], yr.at[0], 15, y_up),
    ]
    halo_x = [send_x(t0p, 10), send_x(wp, 12)]

    for name in ("cell", "loc", "ext"):
        loads[name].wait()
    loads["mark"].wait()
    cell_row = cell[...] >> 8
    oh_lane[...] = one_hot((cell[...] & (NZ - 1)).astype(F32).astype(BF16), column[...], NZ)
    row_c[...] = cell_row
    row, lane = decode(loc[...], gx, zh)
    row_a[...], lane_a[...] = row, lane.astype(F32)
    slot = lax.broadcasted_iota(I32, (1, SLOTS), 1)
    ext[...] = jnp.where(slot < active[0], ext[...], 0.0)
    for name in ("f0", "st", "pe"):
        loads[name].wait()

    visits = []
    group, window = jnp.int32(0), jnp.int32(0)
    for _ in range(VISITS):
        over = group >= GROUPS
        at = jnp.minimum(group, GROUPS - 1)
        visits.append((at, window, jnp.where(over, -1, window * WIDTH)))
        last = mark[0, at * GROUP + (GROUP - 1)] >> 8
        more = jnp.logical_and(last >= (window + 1) * WIDTH, jnp.logical_not(over))
        window = jnp.where(more, window + 1, window)
        group = jnp.where(more, group, group + 1)

    for k in range(GROUPS):
        oh_group[k] = oh_lane[:, k * GROUP : (k + 1) * GROUP]
        row_group[k] = row_c[:, k * GROUP : (k + 1) * GROUP]

    def put(k, i, x):
        high, low = halves(x)
        rows = pl.ds(pl.multiple_of(lax.rem(i, 2) * NY, NY), NY)
        fmat[i // 2, k, rows, 0:NZ] = high
        fmat[i // 2, k, rows, NZ : 2 * NZ] = low

    def pick(fields):
        lo, hi = fields
        count = hi - lo
        found = []
        for at, window, start in visits:
            hot = oh_group[at]
            part = jnp.dot(
                fmat[window, lo:hi].reshape(count * WIDTH, 2 * NZ),
                jnp.concatenate([hot, hot], axis=0),
                preferred_element_type=F32,
            )
            wanted = jnp.where(start < 0, -1, row_group[at] - start)
            hit = row_hit(wanted, WIDTH)
            found.append(
                [
                    jnp.sum(
                        jnp.where(hit, part[f * WIDTH : (f + 1) * WIDTH], 0.0),
                        axis=0,
                        keepdims=True,
                    )
                    for f in range(count)
                ]
            )
        for k in range(GROUPS):
            for f in range(count):
                total = jnp.zeros((1, GROUP), F32)
                for (at, _, _), values in zip(visits, found):
                    total = total + jnp.where(at == k, values[f], 0.0)
                fv[lo + f, :, k * GROUP : (k + 1) * GROUP] = total

    @pl.loop(0, NX, unroll=2)
    def _(i):
        t, tw = t0p[i + 1], te[i]
        lifted = t - bath
        growth = rate(st[i]) * (1.0 - f0[i]) * gate(t)
        new = f0[i] + growth
        f1[i] = new
        tb[i] = enthalpy * growth
        slope = (enthalpy * tw + pe[i]) * (rate(st[i]) * (1.0 - new)) * -sharpness
        put(0, i, lifted)
        put(1, i, tw * lifted)
        put(2, i, slope * lifted)

    def gather(matrix, size, hot, row, out):
        found = jnp.dot(
            matrix[...], jnp.concatenate([hot, hot], axis=0), preferred_element_type=F32
        )
        found = jnp.where(row_hit(row, size), found, 0.0)
        out[...] = jnp.sum(found, axis=0, keepdims=True)

    def scatter(value, size, hot, row):
        high, low = halves(value)
        right = jnp.concatenate(
            [hot * jnp.broadcast_to(high, hot.shape), hot * jnp.broadcast_to(low, hot.shape)],
            axis=1,
        )
        left = jnp.where(row_hit(row, size), 1.0, 0.0).astype(BF16)
        return lax.dot_general(
            jnp.concatenate([left, left], axis=1),
            right,
            (((1,), (1,)), ((), ())),
            preferred_element_type=F32,
        )

    def hot_lanes(ref):
        return one_hot(ref[...].astype(BF16), column[...], 256)

    pick((0, 3))
    fv[0] = ext[...] * fv[0]
    fv[1] = ext[...] * (ext[...] * fv[1])
    fv[2] = ext[...] * fv[2]
    early = send(fv.at[pl.ds(0, 3)], pfv.at[pl.ds(0, 3)], 17, partner)

    def slot_gradient(value, kept):
        g = gate(kept[3] - value * kept[0])
        return 2.0 * value * kept[1] - kept[4] - kept[2] * (g * (1.0 - g))


    loads["coef"].wait()
    for copy in table:
        copy.wait_recv()
    pieces = []
    for part in range(2):
        pieces.append(halves(tab[:, part].reshape(HROWS, 128)))
    tmat[...] = jnp.concatenate(
        [pieces[0][0], pieces[1][0], pieces[0][1], pieces[1][1]], axis=1
    )

    request.wait_recv()
    row, lane = decode(ploc[...], gx, zh)
    row_b[...], lane_b[...] = row, lane.astype(F32)
    gather(tmat, HROWS, hot_lanes(lane_b), row_b[...], val_b)
    reply = send(val_b, ret, 16, partner)

    for copy in halo:
        copy.wait_recv()
    for arrived in halo_x:
        arrived()
    outer.wait_recv()
    yr[0] = jnp.where(gy > 0, yr[0], 0.0)
    yr[1] = jnp.where(gy < 3, yr[1], 0.0)

    def z_halo(inner, outer):
        outer = jnp.where(outer_live, outer, 0.0)
        return z_block(jnp.where(even, outer, inner), jnp.where(even, inner, outer))

    for k in range(2):
        zt[k] = z_halo(zr[0, k : k + 1], zr[1, k : k + 1])

    @pl.loop(0, NX, unroll=2)
    def _(i):
        t = t0p[i + 1]
        around = neighbours(t, t0p[i], t0p[i + 2], yr[0, 0, i], yr[1, 0, i], zt[0, i])
        adjoint = neighbours(wp[i + 1], wp[i], wp[i + 2], yr[0, 1, i], yr[1, 1, i], zt[1, i])
        d, tw = dn[i], te[i]
        plain = t + d * (around - 6.0 * t) + tb[i]
        tb[i] = plain
        put(3, i, plain)
        put(4, i, tw * (plain - bath) + (tw * (1.0 - 6.0 * d) + adjoint) * (t - bath))

    pick((3, 5))
    fv[4] = ext[...] * fv[4]
    late = send(fv.at[pl.ds(3, 2)], pfv.at[pl.ds(3, 2)], 31, partner)
    gather(tmat, HROWS, hot_lanes(lane_a), row_a[...], val_a)

    sg[...] = slot_gradient(val_a[...], fv)
    acc[...] = scatter(sg[...], HROWS, hot_lanes(lane_a), row_a[...])

    reply.wait_recv()
    val_a[...] = ext[...] * (val_a[...] + ret[...])
    sink[...] = scatter(val_a[...], ROWS, oh_lane[...], row_c[...])

    @pl.loop(0, NX, unroll=4)
    def _(i):
        rows = pl.ds(pl.multiple_of(i * NY, NY), NY)
        t1p[i + 1] = tb[i] - sink[rows, :] * (t0p[i + 1] - bath)

    ys1[0] = t1p[1:17, 0:1, :]
    ys1[1] = t1p[1:17, NY - 1 : NY, :]
    left, right = z_faces(t1p[1:17])
    zs1[0] = jnp.where(even, right, left)
    zs1[1] = jnp.where(even, left, right)
    halo = [
        send(zs1.at[1], zr1.at[1], 18, partner),
        send(zs1.at[0], zr1.at[0], 19, mate),
        send(ys1.at[0], yr1.at[1], 22, y_down),
        send(ys1.at[1], yr1.at[0], 23, y_up),
    ]
    halo_x = send_x(t1p, 20)
    early.wait_recv()
    late.wait_recv()
    psg[...] = slot_gradient(val_b[...], pfv)
    acc[...] += scatter(psg[...], HROWS, hot_lanes(lane_b), row_b[...])
    for g in range(4):
        for part in range(2):
            spread[g, part] = acc[g * CROWS : (g + 1) * CROWS, part * 128 : (part + 1) * 128]
    shares = [
        send(spread.at[pgy, pc], rs.at[j], 23 + j, device) for j, pgy, pc, device in peers
    ]

    @pl.loop(0, NX, unroll=2)
    def _(i):
        rows = pl.ds(pl.multiple_of(i * NY, NY), NY)
        drain = sink[rows, :]
        t1 = t1p[i + 1]
        growth = rate(st[i]) * (1.0 - f1[i]) * gate(t1)
        f2[i] = f1[i] + growth
        t2[i] = t1 - 6.0 * dn[i] * t1 + enthalpy * growth - drain * (t1 - bath)

    for copy in halo:
        copy.wait_recv()
    halo_x()
    yr1[0] = jnp.where(gy > 0, yr1[0], 0.0)
    yr1[1] = jnp.where(gy < 3, yr1[1], 0.0)
    zt[0] = z_halo(zr1[0], zr1[1])

    @pl.loop(0, NX, unroll=4)
    def _(i):
        around = neighbours(
            t1p[i + 1], t1p[i], t1p[i + 2], yr1[0, i], yr1[1, i], zt[0, i]
        )
        t2[i] = t2[i] + dn[i] * around

    total = spread[gy, c]
    for copy, (j, _, _, _) in zip(shares, peers):
        copy.wait_recv()
        total = total + rs[j]
    sens[...] = total
    for wait in sent:
        wait()


def deliver(t2, f2, sens, temp_out, frac_out, sens_out, sem):
    copies = [
        pltpu.make_async_copy(source, target, sem.at[k])
        for k, (source, target) in enumerate(((t2, temp_out), (f2, frac_out), (sens, sens_out)))
    ]
    for copy in copies:
        copy.start()
    for copy in copies:
        copy.wait()


def on_device(t0, f0, dn, st, coef, cell, loc, ext, active, te, pe):
    field = (NX, NY, NZ)
    padded = (NX + 2, NY, NZ)
    row = (1, SLOTS)
    vmem = pltpu.VMEM
    anywhere = pl.BlockSpec(memory_space=pl.ANY)
    scratch = (
        [vmem(padded, F32)] * 3
        + [vmem(field, F32)] * 2
        + [vmem(field, I32)]
        + [vmem(field, F32)] * 4
        + [
            vmem((4, 2, CROWS, 128), F32),
            vmem((8, CROWS, 128), F32),
            vmem((4, 2, CROWS, 128), F32),
            vmem(row, I32),
            pltpu.SMEM(row, I32),
            vmem(row, I32),
            vmem(row, I32),
            vmem(row, F32),
        ]
        + [vmem(row, I32)]
        + [vmem(row, F32), vmem(row, I32)] * 2
        + [vmem(row, F32)] * 5
        + [vmem((2, 2, NX, 1, NZ), F32)] * 2
        + [vmem((2, NX, 1, NZ), F32)] * 2
        + [vmem((2, 2, ROWS), F32)] * 2
        + [vmem((2, 1, ROWS), F32)] * 2
        + [
            vmem((2, NX, NY, 128), F32),
            vmem((ROWS, NZ), F32),
            vmem((HROWS, 256), F32),
            vmem((HROWS, 512), BF16),
            vmem((WINDOWS, 5, WIDTH, 512), BF16),
            vmem((5, 1, SLOTS), F32),
            vmem((5, 1, SLOTS), F32),
            vmem((NZ, SLOTS), BF16),
            vmem((GROUPS, NZ, GROUP), BF16),
            vmem((GROUPS, 1, GROUP), I32),
            vmem((256, 128), BF16),
            pltpu.SemaphoreType.DMA((11,)),
            pltpu.SemaphoreType.DMA((32,)),
            pltpu.SemaphoreType.DMA((32,)),
        ]
    )
    results = (
        jax.ShapeDtypeStruct(field, F32),
        jax.ShapeDtypeStruct(field, F32),
        jax.ShapeDtypeStruct((CROWS, 128), F32),
    )
    done = pl.pallas_call(
        kernel,
        out_shape=(vmem(field, F32), vmem(field, F32), vmem((CROWS, 128), F32)),
        in_specs=[pl.BlockSpec(memory_space=pltpu.SMEM)] + [anywhere] * 10,
        out_specs=(pl.BlockSpec(memory_space=vmem),) * 3,
        scratch_shapes=scratch,
        compiler_params=pltpu.CompilerParams(
            collective_id=0, has_side_effects=True, vmem_limit_bytes=56 * 2**20
        ),
    )(
        active,
        t0,
        f0,
        dn,
        st,
        coef.reshape(CROWS, 128),
        cell.reshape(row),
        loc.reshape(row),
        ext.reshape(row),
        te,
        pe,
    )
    temp, frac, sens = pl.pallas_call(
        deliver,
        out_shape=results,
        in_specs=[anywhere] * 3,
        out_specs=(anywhere,) * 3,
        scratch_shapes=[pltpu.SemaphoreType.DMA((3,))],
        compiler_params=pltpu.CompilerParams(vmem_limit_bytes=2**20),
    )(*done)
    return temp, frac, sens.reshape(CHUNK)


def solution(mesh):
    brick, line = P("gx", "gy", "gz"), P(("gx", "gy", "gz"))
    return jax.shard_map(
        on_device,
        mesh=mesh,
        in_specs=(brick,) * 4 + (line,) * 5 + (brick,) * 2,
        out_specs=(brick, brick, line),
        check_vma=False,
    )
```

```python
import functools

import jax
import jax.numpy as jnp
from jax import lax
from jax.experimental import pallas as pl
from jax.experimental.pallas import tpu as pltpu
from jax.sharding import PartitionSpec as P

MESH = pl.DeviceIdType.MESH
F32 = jnp.float32
BF16 = jnp.bfloat16
I32 = jnp.int32

NX, NY, NZ = 16, 32, 256
ROWS = NX * NY
SLOTS = 2048
CHUNK = 7168
CROWS = CHUNK // 128
HROWS = 4 * CROWS
SLAB = 16 * CHUNK
GROUP = 256
GROUPS = SLOTS // GROUP
WIDTH = 64
WINDOWS = ROWS // WIDTH
VISITS = GROUPS + WINDOWS - 1
TALL = 128
TALL_WINDOWS = ROWS // TALL
TALL_VISITS = GROUPS + TALL_WINDOWS - 1

sharpness = 4.0
kinetic_fast = 0.6
kinetic_slow = 0.2
enthalpy = 0.4
bath = -2.0


def halves(x):
    high = x.astype(BF16)
    return high, (x - high.astype(F32)).astype(BF16)


def one_hot(index, column, size):
    column = jnp.concatenate([column] * (index.shape[1] // 128), axis=1)
    hit = column == jnp.broadcast_to(index, (size, index.shape[1]))
    return jnp.where(hit, jnp.ones((), BF16), jnp.zeros((), BF16))


def row_hit(index, size):
    rows = lax.broadcasted_iota(I32, (size, index.shape[1]), 0)
    return rows == index


def gate(t):
    return jax.nn.sigmoid(sharpness * (0.0 - t))


def rate(status):
    return jnp.where(status == 1, kinetic_fast, jnp.where(status == 2, kinetic_slow, 0.0))


def decode(loc, gx, zh):
    local = loc - gx * SLAB
    row = local >> 7
    owner = (row * 1171) >> 16
    inner = row - owner * CROWS
    mine = ((owner >> 1) & 1) == zh
    return jnp.where(mine, (owner >> 2) * CROWS + inner, -1), (owner & 1) * 128 + (local & 127)


def neighbours(center, low, high, y_low, y_high, z_edge):
    y = lax.broadcasted_iota(I32, (NY, NZ), 0)
    z = lax.broadcasted_iota(I32, (NY, NZ), 1)
    edge = jnp.concatenate([z_edge, z_edge], axis=1)
    total = low + high
    total = total + jnp.where(y == 0, y_low, pltpu.roll(center, 1, 0))
    total = total + jnp.where(y == NY - 1, y_high, pltpu.roll(center, NY - 1, 0))
    total = total + jnp.where(z == 0, edge, pltpu.roll(center, 1, 1))
    return total + jnp.where(z == NZ - 1, edge, pltpu.roll(center, NZ - 1, 1))


def z_faces(x):
    x = x.reshape(ROWS, NZ)
    lane = lax.broadcasted_iota(I32, (ROWS, 128), 1)
    both = jnp.where(lane == 0, x[:, :128], x[:, 128:]).T
    return both[0:1, :], both[127:128, :]


def z_block(left, right):
    row = lax.broadcasted_iota(I32, (128, ROWS), 0)
    both = jnp.where(row == 0, left, jnp.where(row == 127, right, 0.0))
    return both.T.reshape(NX, NY, 128)


def kernel(
    live_hbm,
    t0_hbm,
    f0_hbm,
    dn_hbm,
    st_hbm,
    coef_hbm,
    cell_hbm,
    loc_hbm,
    ext_hbm,
    te_hbm,
    pe_hbm,
    t2,
    f2,
    sens,
    t0p,
    wp,
    t1p,
    f0,
    dn,
    st,
    te,
    pe,
    tb,
    f1,
    tab,
    rs,
    spread,
    active,
    cell,
    mark,
    loc,
    ploc,
    ext,
    row_c,
    lane_a,
    row_a,
    lane_b,
    row_b,
    val_a,
    val_b,
    ret,
    sg,
    psg,
    ys,
    yr,
    ys1,
    yr1,
    zs,
    zr,
    zs1,
    zr1,
    zt,
    sink,
    acc,
    tmat,
    fmat,
    fv,
    pfv,
    hot_a,
    hot_b,
    left_b,
    rises,
    slopes,
    oh_lane,
    oh_group,
    row_group,
    column,
    load_sem,
    send_sem,
    recv_sem,
):
    gx, gy, gz = lax.axis_index("gx"), lax.axis_index("gy"), lax.axis_index("gz")
    zh, c = gz // 2, gz % 2
    even = c == 0
    outer_live = jnp.logical_or(gz == 1, gz == 2)
    partner = (gx, gy, 3 - gz)
    mate = (gx, gy, zh * 2 + (1 - c))
    x_up, x_down = (jnp.minimum(gx + 1, 15), gy, gz), (jnp.maximum(gx - 1, 0), gy, gz)
    has_up, has_down = gx < 15, gx > 0
    y_up, y_down = (gx, lax.rem(gy + 1, 4), gz), (gx, lax.rem(gy + 3, 4), gz)
    peers = []
    for j in (4, 5, 2, 3, 6, 7, 1):
        pgy, pc = lax.rem(gy + j // 2, 4), lax.rem(c + j % 2, 2)
        peers.append((j, pgy, pc, (gx, pgy, zh * 2 + pc)))

    barrier = pltpu.get_barrier_semaphore()

    def greet(device):
        pl.semaphore_signal(barrier, inc=1, device_id=device, device_id_type=MESH)

    greet(partner)
    pl.when(has_up)(lambda: greet(x_up))
    pl.when(has_down)(lambda: greet(x_down))
    for _, _, _, device in peers:
        greet(device)
    expected = 7 + has_up.astype(I32) + has_down.astype(I32) + 1

    loads = {}
    for k, (name, source, target) in enumerate(
        (
            ("t0", t0_hbm, t0p.at[pl.ds(1, NX)]),
            ("dn", dn_hbm, dn),
            ("te", te_hbm, te),
            ("cell", cell_hbm, cell),
            ("mark", cell_hbm, mark),
            ("active", live_hbm, active),
            ("loc", loc_hbm, loc),
            ("ext", ext_hbm, ext),
            ("coef", coef_hbm, tab.at[gy, c]),
            ("f0", f0_hbm, f0),
            ("st", st_hbm, st),
            ("pe", pe_hbm, pe),
        )
    ):
        loads[name] = pltpu.make_async_copy(source, target, load_sem.at[k])
        loads[name].start()

    sent = []

    def remote(source, target, index, device):
        return pltpu.make_async_remote_copy(
            src_ref=source,
            dst_ref=target,
            send_sem=send_sem.at[index],
            recv_sem=recv_sem.at[index],
            device_id=device,
            device_id_type=MESH,
        )

    def send(source, target, index, device):
        copy = remote(source, target, index, device)
        copy.start()
        sent.append(copy.wait_send)
        return copy

    def send_x(padded, index):
        down = remote(padded.at[1], padded.at[NX + 1], index, x_down)
        up = remote(padded.at[NX], padded.at[0], index + 1, x_up)
        pl.when(has_down)(down.start)
        pl.when(has_up)(up.start)
        sent.append(lambda: pl.when(has_down)(down.wait_send))
        sent.append(lambda: pl.when(has_up)(up.wait_send))

        def arrived():
            pl.when(has_up)(down.wait_recv)
            pl.when(has_down)(up.wait_recv)
            padded[0] = jnp.where(has_down, padded[0], 0.0)
            padded[NX + 1] = jnp.where(has_up, padded[NX + 1], 0.0)

        return arrived

    base = lax.broadcasted_iota(I32, (256, 128), 0).astype(F32).astype(BF16)
    column[...] = base

    loads["t0"].wait()
    loads["dn"].wait()
    loads["te"].wait()

    @pl.loop(0, NX, unroll=2)
    def _(i):
        wp[i + 1] = dn[i] * te[i]

    for k, padded in enumerate((t0p, wp)):
        ys[0, k] = padded[1:17, 0:1, :]
        ys[1, k] = padded[1:17, NY - 1 : NY, :]
        left, right = z_faces(padded[1:17])
        zs[0, k : k + 1] = jnp.where(even, right, left)
        zs[1, k : k + 1] = jnp.where(even, left, right)

    pl.semaphore_wait(barrier, expected)
    request = send(loc_hbm, ploc, 0, partner)
    outer = send(zs.at[1], zr.at[1], 8, partner)
    table = [send(coef_hbm, tab.at[gy, c], j, device) for j, _, _, device in peers]
    halo = [
        send(zs.at[0], zr.at[0], 9, mate),
        send(ys.at[0], yr.at[1], 14, y_down),
        send(ys.at[1], yr.at[0], 15, y_up),
    ]
    halo_x = [send_x(t0p, 10), send_x(wp, 12)]

    for name in ("cell", "loc", "ext"):
        loads[name].wait()
    loads["mark"].wait()
    loads["active"].wait()
    cell_row = cell[...] >> 8
    oh_lane[...] = one_hot((cell[...] & (NZ - 1)).astype(F32).astype(BF16), column[...], NZ)
    row_c[...] = cell_row
    row, lane = decode(loc[...], gx, zh)
    row_a[...], lane_a[...] = row, lane.astype(F32)
    slot = lax.broadcasted_iota(I32, (1, SLOTS), 1)
    ext[...] = jnp.where(slot < active[0], ext[...], 0.0)
    for name in ("f0", "st", "pe"):
        loads[name].wait()

    def path(count, width):
        visits = []
        group, window = jnp.int32(0), jnp.int32(0)
        for _ in range(count):
            over = group >= GROUPS
            at = jnp.minimum(group, GROUPS - 1)
            visits.append((at, window, jnp.where(over, -1, window * width)))
            last = mark[0, at * GROUP + (GROUP - 1)] >> 8
            more = jnp.logical_and(last >= (window + 1) * width, jnp.logical_not(over))
            window = jnp.where(more, window + 1, window)
            group = jnp.where(more, group, group + 1)
        return visits

    visits, tall = path(VISITS, WIDTH), path(TALL_VISITS, TALL)

    for k in range(GROUPS):
        oh_group[k] = oh_lane[:, k * GROUP : (k + 1) * GROUP]
        row_group[k] = row_c[:, k * GROUP : (k + 1) * GROUP]

    ends = [jnp.int32(TALL_VISITS)] * TALL_WINDOWS
    for k, (at, window, start) in enumerate(tall):
        wanted = jnp.where(start < 0, -1, row_group[at] - start)
        rises[k] = jnp.where(row_hit(wanted, TALL), 1.0, 0.0).astype(BF16)
        ends = [jnp.where(window == w, k, end) for w, end in enumerate(ends)]
    sink[TALL_VISITS] = jnp.zeros((TALL, NZ), F32)

    def put(k, i, x):
        high, low = halves(x)
        rows = pl.ds(pl.multiple_of(lax.rem(i, 2) * NY, NY), NY)
        fmat[i // 2, k, rows, 0:NZ] = high
        fmat[i // 2, k, rows, NZ : 2 * NZ] = low

    def pick(fields):
        lo, hi = fields
        count = hi - lo
        found = []
        for at, window, start in visits:
            hot = oh_group[at]
            part = jnp.dot(
                fmat[window, lo:hi].reshape(count * WIDTH, 2 * NZ),
                jnp.concatenate([hot, hot], axis=0),
                preferred_element_type=F32,
            )
            wanted = jnp.where(start < 0, -1, row_group[at] - start)
            hit = row_hit(wanted, WIDTH)
            found.append(
                [
                    jnp.sum(
                        jnp.where(hit, part[f * WIDTH : (f + 1) * WIDTH], 0.0),
                        axis=0,
                        keepdims=True,
                    )
                    for f in range(count)
                ]
            )
        for k in range(GROUPS):
            for f in range(count):
                total = jnp.zeros((1, GROUP), F32)
                for (at, _, _), values in zip(visits, found):
                    total = total + jnp.where(at == k, values[f], 0.0)
                fv[lo + f, :, k * GROUP : (k + 1) * GROUP] = total

    @pl.loop(0, NX, unroll=2)
    def _(i):
        t, tw = t0p[i + 1], te[i]
        lifted = t - bath
        growth = rate(st[i]) * (1.0 - f0[i]) * gate(t)
        new = f0[i] + growth
        f1[i] = new
        tb[i] = enthalpy * growth
        slope = (enthalpy * tw + pe[i]) * (rate(st[i]) * (1.0 - new)) * -sharpness
        put(0, i, lifted)
        put(1, i, tw * lifted)
        put(2, i, slope * lifted)

    def gather(matrix, size, hot, row, out):
        found = jnp.dot(
            matrix[...], jnp.concatenate([hot, hot], axis=0), preferred_element_type=F32
        )
        found = jnp.where(row_hit(row, size), found, 0.0)
        out[...] = jnp.sum(found, axis=0, keepdims=True)

    def scatter(value, hot, left):
        high, low = halves(value)
        right = jnp.concatenate(
            [hot * jnp.broadcast_to(high, hot.shape), hot * jnp.broadcast_to(low, hot.shape)],
            axis=1,
        )
        return lax.dot_general(
            jnp.concatenate([left, left], axis=1),
            right,
            (((1,), (1,)), ((), ())),
            preferred_element_type=F32,
        )

    def row_marks(ref):
        return jnp.where(row_hit(ref[...], HROWS), 1.0, 0.0).astype(BF16)

    def hot_lanes(ref):
        return one_hot(ref[...].astype(BF16), column[...], 256)

    pick((0, 3))
    fv[0] = ext[...] * fv[0]
    fv[1] = ext[...] * (ext[...] * fv[1])
    fv[2] = ext[...] * fv[2]
    early = send(fv.at[pl.ds(0, 3)], pfv.at[pl.ds(0, 3)], 17, partner)

    def slot_gradient(value, kept):
        g = gate(kept[3] - value * kept[0])
        return 2.0 * value * kept[1] - kept[4] - kept[2] * (g * (1.0 - g))


    loads["coef"].wait()
    for copy in table:
        copy.wait_recv()
    pieces = []
    for part in range(2):
        pieces.append(halves(tab[:, part].reshape(HROWS, 128)))
    tmat[...] = jnp.concatenate(
        [pieces[0][0], pieces[1][0], pieces[0][1], pieces[1][1]], axis=1
    )

    request.wait_recv()
    row, lane = decode(ploc[...], gx, zh)
    row_b[...], lane_b[...] = row, lane.astype(F32)
    hot_b[...] = hot_lanes(lane_b)
    gather(tmat, HROWS, hot_b[...], row_b[...], val_b)
    reply = send(val_b, ret, 16, partner)

    for copy in halo:
        copy.wait_recv()
    for arrived in halo_x:
        arrived()
    outer.wait_recv()
    yr[0] = jnp.where(gy > 0, yr[0], 0.0)
    yr[1] = jnp.where(gy < 3, yr[1], 0.0)

    def z_halo(inner, outer):
        outer = jnp.where(outer_live, outer, 0.0)
        return z_block(jnp.where(even, outer, inner), jnp.where(even, inner, outer))

    for k in range(2):
        zt[k] = z_halo(zr[0, k : k + 1], zr[1, k : k + 1])

    @pl.loop(0, NX, unroll=2)
    def _(i):
        t = t0p[i + 1]
        around = neighbours(t, t0p[i], t0p[i + 2], yr[0, 0, i], yr[1, 0, i], zt[0, i])
        adjoint = neighbours(wp[i + 1], wp[i], wp[i + 2], yr[0, 1, i], yr[1, 1, i], zt[1, i])
        d, tw = dn[i], te[i]
        plain = t + d * (around - 6.0 * t) + tb[i]
        tb[i] = plain
        put(3, i, plain)
        put(4, i, tw * (plain - bath) + (tw * (1.0 - 6.0 * d) + adjoint) * (t - bath))

    pick((3, 5))
    fv[4] = ext[...] * fv[4]
    late = send(fv.at[pl.ds(3, 2)], pfv.at[pl.ds(3, 2)], 31, partner)
    hot_a[...] = hot_lanes(lane_a)
    gather(tmat, HROWS, hot_a[...], row_a[...], val_a)

    sg[...] = slot_gradient(val_a[...], fv)
    acc[...] = scatter(sg[...], hot_a[...], row_marks(row_a))
    left_b[...] = row_marks(row_b)

    reply.wait_recv()
    val_a[...] = ext[...] * (val_a[...] + ret[...])
    high, low = halves(val_a[...])
    for k in range(GROUPS):
        cols = slice(k * GROUP, (k + 1) * GROUP)
        hot = oh_group[k]
        slopes[k, :, 0:GROUP] = hot * jnp.broadcast_to(high[:, cols], hot.shape)
        slopes[k, :, GROUP : 2 * GROUP] = hot * jnp.broadcast_to(low[:, cols], hot.shape)
    running = None
    for k, (at, window, _) in enumerate(tall):
        rise = rises[k]
        part = lax.dot_general(
            jnp.concatenate([rise, rise], axis=1),
            slopes[at],
            (((1,), (1,)), ((), ())),
            preferred_element_type=F32,
        )
        if k:
            part = part + jnp.where(window == tall[k - 1][1], running, 0.0)
        sink[k] = part
        running = part

    per = TALL // NY
    for w, end in enumerate(ends):
        for k in range(per):
            i = w * per + k
            drain = sink[end, k * NY : (k + 1) * NY, :]
            t1p[i + 1] = tb[i] - drain * (t0p[i + 1] - bath)

    ys1[0] = t1p[1:17, 0:1, :]
    ys1[1] = t1p[1:17, NY - 1 : NY, :]
    left, right = z_faces(t1p[1:17])
    zs1[0] = jnp.where(even, right, left)
    zs1[1] = jnp.where(even, left, right)
    halo = [
        send(zs1.at[1], zr1.at[1], 18, partner),
        send(zs1.at[0], zr1.at[0], 19, mate),
        send(ys1.at[0], yr1.at[1], 22, y_down),
        send(ys1.at[1], yr1.at[0], 23, y_up),
    ]
    halo_x = send_x(t1p, 20)
    early.wait_recv()
    late.wait_recv()
    psg[...] = slot_gradient(val_b[...], pfv)
    acc[...] += scatter(psg[...], hot_b[...], left_b[...])
    for g in range(4):
        for part in range(2):
            spread[g, part] = acc[g * CROWS : (g + 1) * CROWS, part * 128 : (part + 1) * 128]
    shares = [
        send(spread.at[pgy, pc], rs.at[j], 23 + j, device) for j, pgy, pc, device in peers
    ]

    for w, end in enumerate(ends):

        @pl.loop(0, per, unroll=2)
        def _(k):
            i = w * per + k
            drain = sink[end, pl.ds(pl.multiple_of(k * NY, NY), NY), :]
            t1 = t1p[i + 1]
            growth = rate(st[i]) * (1.0 - f1[i]) * gate(t1)
            f2[i] = f1[i] + growth
            t2[i] = t1 - 6.0 * dn[i] * t1 + enthalpy * growth - drain * (t1 - bath)

    for copy in halo[1:]:
        copy.wait_recv()
    halo_x()
    yr1[0] = jnp.where(gy > 0, yr1[0], 0.0)
    yr1[1] = jnp.where(gy < 3, yr1[1], 0.0)
    zt[0] = z_halo(zr1[0], jnp.zeros((1, ROWS), F32))

    @pl.loop(0, NX, unroll=4)
    def _(i):
        around = neighbours(
            t1p[i + 1], t1p[i], t1p[i + 2], yr1[0, i], yr1[1, i], zt[0, i]
        )
        t2[i] = t2[i] + dn[i] * around

    halo[0].wait_recv()
    outside = jnp.where(outer_live, zr1[1], 0.0)
    outside = z_block(jnp.where(even, outside, 0.0), jnp.where(even, 0.0, outside))
    tile = pl.ds(pl.multiple_of((1 - even.astype(I32)) * 128, 128), 128)
    t2[:, :, tile] = t2[:, :, tile] + dn[:, :, tile] * outside

    total = spread[gy, c]
    for copy, (j, _, _, _) in zip(shares, peers):
        copy.wait_recv()
        total = total + rs[j]
    sens[...] = total
    for wait in sent:
        wait()


def deliver(t2, f2, sens, temp_out, frac_out, sens_out, sem):
    copies = [
        pltpu.make_async_copy(source, target, sem.at[k])
        for k, (source, target) in enumerate(((t2, temp_out), (f2, frac_out), (sens, sens_out)))
    ]
    for copy in copies:
        copy.start()
    for copy in copies:
        copy.wait()


def on_device(t0, f0, dn, st, coef, cell, loc, ext, active, te, pe):
    field = (NX, NY, NZ)
    padded = (NX + 2, NY, NZ)
    row = (1, SLOTS)
    vmem = pltpu.VMEM
    anywhere = pl.BlockSpec(memory_space=pl.ANY)
    scratch = (
        [vmem(padded, F32)] * 3
        + [vmem(field, F32)] * 2
        + [vmem(field, I32)]
        + [vmem(field, F32)] * 4
        + [
            vmem((4, 2, CROWS, 128), F32),
            vmem((8, CROWS, 128), F32),
            vmem((4, 2, CROWS, 128), F32),
            pltpu.SMEM((1,), I32),
            vmem(row, I32),
            pltpu.SMEM(row, I32),
            vmem(row, I32),
            vmem(row, I32),
            vmem(row, F32),
        ]
        + [vmem(row, I32)]
        + [vmem(row, F32), vmem(row, I32)] * 2
        + [vmem(row, F32)] * 5
        + [vmem((2, 2, NX, 1, NZ), F32)] * 2
        + [vmem((2, NX, 1, NZ), F32)] * 2
        + [vmem((2, 2, ROWS), F32)] * 2
        + [vmem((2, 1, ROWS), F32)] * 2
        + [
            vmem((2, NX, NY, 128), F32),
            vmem((TALL_VISITS + 1, TALL, NZ), F32),
            vmem((HROWS, 256), F32),
            vmem((HROWS, 512), BF16),
            vmem((WINDOWS, 5, WIDTH, 512), BF16),
            vmem((5, 1, SLOTS), F32),
            vmem((5, 1, SLOTS), F32),
            vmem((256, SLOTS), BF16),
            vmem((256, SLOTS), BF16),
            vmem((HROWS, SLOTS), BF16),
            vmem((TALL_VISITS, TALL, GROUP), BF16),
            vmem((GROUPS, NZ, 2 * GROUP), BF16),
            vmem((NZ, SLOTS), BF16),
            vmem((GROUPS, NZ, GROUP), BF16),
            vmem((GROUPS, 1, GROUP), I32),
            vmem((256, 128), BF16),
            pltpu.SemaphoreType.DMA((12,)),
            pltpu.SemaphoreType.DMA((32,)),
            pltpu.SemaphoreType.DMA((32,)),
        ]
    )
    results = (
        jax.ShapeDtypeStruct(field, F32),
        jax.ShapeDtypeStruct(field, F32),
        jax.ShapeDtypeStruct((CROWS, 128), F32),
    )
    done = pl.pallas_call(
        kernel,
        out_shape=(vmem(field, F32), vmem(field, F32), vmem((CROWS, 128), F32)),
        in_specs=[anywhere] * 11,
        out_specs=(pl.BlockSpec(memory_space=vmem),) * 3,
        scratch_shapes=scratch,
        compiler_params=pltpu.CompilerParams(
            collective_id=0, has_side_effects=True, vmem_limit_bytes=56 * 2**20
        ),
    )(
        active,
        t0,
        f0,
        dn,
        st,
        coef.reshape(CROWS, 128),
        cell.reshape(row),
        loc.reshape(row),
        ext.reshape(row),
        te,
        pe,
    )
    temp, frac, sens = pl.pallas_call(
        deliver,
        out_shape=results,
        in_specs=[anywhere] * 3,
        out_specs=(anywhere,) * 3,
        scratch_shapes=[pltpu.SemaphoreType.DMA((3,))],
        compiler_params=pltpu.CompilerParams(vmem_limit_bytes=2**20),
    )(*done)
    return temp, frac, sens.reshape(CHUNK)


def solution(mesh):
    brick, line = P("gx", "gy", "gz"), P(("gx", "gy", "gz"))
    return jax.shard_map(
        on_device,
        mesh=mesh,
        in_specs=(brick,) * 4 + (line,) * 5 + (brick,) * 2,
        out_specs=(brick, brick, line),
        check_vma=False,
    )
```

```python
import functools

import jax
import jax.numpy as jnp
from jax import lax
from jax.experimental import pallas as pl
from jax.experimental.pallas import tpu as pltpu
from jax.sharding import PartitionSpec as P

MESH = pl.DeviceIdType.MESH
F32 = jnp.float32
BF16 = jnp.bfloat16
I32 = jnp.int32

NX, NY, NZ = 16, 32, 256
ROWS = NX * NY
SLOTS = 2048
CHUNK = 7168
CROWS = CHUNK // 128
HROWS = 4 * CROWS
SLAB = 16 * CHUNK
GROUP = 256
GROUPS = SLOTS // GROUP
WIDTH = 64
WINDOWS = ROWS // WIDTH
VISITS = GROUPS + WINDOWS - 1
TALL = 128
TALL_WINDOWS = ROWS // TALL
TALL_VISITS = GROUPS + TALL_WINDOWS - 1

sharpness = 4.0
kinetic_fast = 0.6
kinetic_slow = 0.2
enthalpy = 0.4
bath = -2.0


def halves(x):
    high = x.astype(BF16)
    return high, (x - high.astype(F32)).astype(BF16)


def one_hot(index, column, size):
    column = jnp.concatenate([column] * (index.shape[1] // 128), axis=1)
    hit = column == jnp.broadcast_to(index, (size, index.shape[1]))
    return jnp.where(hit, jnp.ones((), BF16), jnp.zeros((), BF16))


def row_hit(index, size):
    rows = lax.broadcasted_iota(I32, (size, index.shape[1]), 0)
    return rows == index


def gate(t):
    return jax.nn.sigmoid(sharpness * (0.0 - t))


def rate(status):
    return jnp.where(status == 1, kinetic_fast, jnp.where(status == 2, kinetic_slow, 0.0))


def decode(loc, gx, zh):
    local = loc - gx * SLAB
    row = local >> 7
    owner = (row * 1171) >> 16
    inner = row - owner * CROWS
    mine = ((owner >> 1) & 1) == zh
    return jnp.where(mine, (owner >> 2) * CROWS + inner, -1), (owner & 1) * 128 + (local & 127)


def neighbours(center, low, high, y_low, y_high, z_edge):
    y = lax.broadcasted_iota(I32, (NY, NZ), 0)
    z = lax.broadcasted_iota(I32, (NY, NZ), 1)
    edge = jnp.concatenate([z_edge, z_edge], axis=1)
    total = low + high
    total = total + jnp.where(y == 0, y_low, pltpu.roll(center, 1, 0))
    total = total + jnp.where(y == NY - 1, y_high, pltpu.roll(center, NY - 1, 0))
    total = total + jnp.where(z == 0, edge, pltpu.roll(center, 1, 1))
    return total + jnp.where(z == NZ - 1, edge, pltpu.roll(center, NZ - 1, 1))


def z_faces(x):
    x = x.reshape(ROWS, NZ)
    lane = lax.broadcasted_iota(I32, (ROWS, 128), 1)
    both = jnp.where(lane == 0, x[:, :128], x[:, 128:]).T
    return both[0:1, :], both[127:128, :]


def z_block(left, right):
    row = lax.broadcasted_iota(I32, (128, ROWS), 0)
    both = jnp.where(row == 0, left, jnp.where(row == 127, right, 0.0))
    return both.T.reshape(NX, NY, 128)


def kernel(
    live_hbm,
    t0_hbm,
    f0_hbm,
    dn_hbm,
    st_hbm,
    coef_hbm,
    cell_hbm,
    loc_hbm,
    ext_hbm,
    te_hbm,
    pe_hbm,
    t2,
    f2,
    sens,
    t0p,
    wp,
    t1p,
    f0,
    dn,
    st,
    te,
    pe,
    tb,
    f1,
    tab,
    rs,
    spread,
    theirs,
    mine,
    active,
    cell,
    mark,
    loc,
    ploc,
    ext,
    row_c,
    lane_a,
    row_a,
    lane_b,
    row_b,
    val_a,
    val_b,
    ret,
    sg,
    psg,
    ys,
    yr,
    ys1,
    yr1,
    zs,
    zr,
    zs1,
    zr1,
    zt,
    sink,
    acc,
    tmat,
    fmat,
    fv,
    pfv,
    hot_a,
    hot_b,
    left_b,
    rises,
    slopes,
    oh_lane,
    oh_group,
    row_group,
    column,
    load_sem,
    send_sem,
    recv_sem,
):
    gx, gy, gz = lax.axis_index("gx"), lax.axis_index("gy"), lax.axis_index("gz")
    zh, c = gz // 2, gz % 2
    even = c == 0
    outer_live = jnp.logical_or(gz == 1, gz == 2)
    partner = (gx, gy, 3 - gz)
    mate = (gx, gy, zh * 2 + (1 - c))
    x_up, x_down = (jnp.minimum(gx + 1, 15), gy, gz), (jnp.maximum(gx - 1, 0), gy, gz)
    has_up, has_down = gx < 15, gx > 0
    y_up, y_down = (gx, lax.rem(gy + 1, 4), gz), (gx, lax.rem(gy + 3, 4), gz)
    peers = []
    for j in (4, 5, 2, 3, 6, 7, 1):
        pgy, pc = lax.rem(gy + j // 2, 4), lax.rem(c + j % 2, 2)
        peers.append((j, pgy, pc, (gx, pgy, zh * 2 + pc)))

    barrier = pltpu.get_barrier_semaphore()

    def greet(device):
        pl.semaphore_signal(barrier, inc=1, device_id=device, device_id_type=MESH)

    greet(partner)
    pl.when(has_up)(lambda: greet(x_up))
    pl.when(has_down)(lambda: greet(x_down))
    for _, _, _, device in peers:
        greet(device)
    expected = 7 + has_up.astype(I32) + has_down.astype(I32) + 1

    loads = {}
    for k, (name, source, target) in enumerate(
        (
            ("t0", t0_hbm, t0p.at[pl.ds(1, NX)]),
            ("dn", dn_hbm, dn),
            ("te", te_hbm, te),
            ("cell", cell_hbm, cell),
            ("mark", cell_hbm, mark),
            ("active", live_hbm, active),
            ("loc", loc_hbm, loc),
            ("ext", ext_hbm, ext),
            ("coef", coef_hbm, tab.at[gy, c]),
            ("f0", f0_hbm, f0),
            ("st", st_hbm, st),
            ("pe", pe_hbm, pe),
        )
    ):
        loads[name] = pltpu.make_async_copy(source, target, load_sem.at[k])
        loads[name].start()

    sent = []

    def remote(source, target, index, device):
        return pltpu.make_async_remote_copy(
            src_ref=source,
            dst_ref=target,
            send_sem=send_sem.at[index],
            recv_sem=recv_sem.at[index],
            device_id=device,
            device_id_type=MESH,
        )

    def send(source, target, index, device):
        copy = remote(source, target, index, device)
        copy.start()
        sent.append(copy.wait_send)
        return copy

    def send_x(padded, index):
        down = remote(padded.at[1], padded.at[NX + 1], index, x_down)
        up = remote(padded.at[NX], padded.at[0], index + 1, x_up)
        pl.when(has_down)(down.start)
        pl.when(has_up)(up.start)
        sent.append(lambda: pl.when(has_down)(down.wait_send))
        sent.append(lambda: pl.when(has_up)(up.wait_send))

        def arrived():
            pl.when(has_up)(down.wait_recv)
            pl.when(has_down)(up.wait_recv)
            padded[0] = jnp.where(has_down, padded[0], 0.0)
            padded[NX + 1] = jnp.where(has_up, padded[NX + 1], 0.0)

        return arrived

    base = lax.broadcasted_iota(I32, (256, 128), 0).astype(F32).astype(BF16)
    column[...] = base

    loads["t0"].wait()
    loads["dn"].wait()
    loads["te"].wait()

    @pl.loop(0, NX, unroll=2)
    def _(i):
        wp[i + 1] = dn[i] * te[i]

    for k, padded in enumerate((t0p, wp)):
        ys[0, k] = padded[1:17, 0:1, :]
        ys[1, k] = padded[1:17, NY - 1 : NY, :]
        left, right = z_faces(padded[1:17])
        zs[0, k : k + 1] = jnp.where(even, right, left)
        zs[1, k : k + 1] = jnp.where(even, left, right)

    pl.semaphore_wait(barrier, expected)
    request = send(loc_hbm, ploc, 0, partner)
    outer = send(zs.at[1], zr.at[1], 8, partner)
    table = [send(coef_hbm, tab.at[gy, c], j, device) for j, _, _, device in peers]
    halo = [
        send(zs.at[0], zr.at[0], 9, mate),
        send(ys.at[0], yr.at[1], 14, y_down),
        send(ys.at[1], yr.at[0], 15, y_up),
    ]
    halo_x = [send_x(t0p, 10), send_x(wp, 12)]

    for name in ("cell", "loc", "ext"):
        loads[name].wait()
    loads["mark"].wait()
    loads["active"].wait()
    cell_row = cell[...] >> 8
    oh_lane[...] = one_hot((cell[...] & (NZ - 1)).astype(F32).astype(BF16), column[...], NZ)
    row_c[...] = cell_row
    row, lane = decode(loc[...], gx, zh)
    row_a[...], lane_a[...] = row, lane.astype(F32)
    slot = lax.broadcasted_iota(I32, (1, SLOTS), 1)
    ext[...] = jnp.where(slot < active[0], ext[...], 0.0)
    for name in ("f0", "st", "pe"):
        loads[name].wait()

    def path(count, width):
        visits = []
        group, window = jnp.int32(0), jnp.int32(0)
        for _ in range(count):
            over = group >= GROUPS
            at = jnp.minimum(group, GROUPS - 1)
            visits.append((at, window, jnp.where(over, -1, window * width)))
            last = mark[0, at * GROUP + (GROUP - 1)] >> 8
            more = jnp.logical_and(last >= (window + 1) * width, jnp.logical_not(over))
            window = jnp.where(more, window + 1, window)
            group = jnp.where(more, group, group + 1)
        return visits

    visits, tall = path(VISITS, WIDTH), path(TALL_VISITS, TALL)

    for k in range(GROUPS):
        oh_group[k] = oh_lane[:, k * GROUP : (k + 1) * GROUP]
        row_group[k] = row_c[:, k * GROUP : (k + 1) * GROUP]

    ends = [jnp.int32(TALL_VISITS)] * TALL_WINDOWS
    for k, (at, window, start) in enumerate(tall):
        wanted = jnp.where(start < 0, -1, row_group[at] - start)
        rises[k] = jnp.where(row_hit(wanted, TALL), 1.0, 0.0).astype(BF16)
        ends = [jnp.where(window == w, k, end) for w, end in enumerate(ends)]
    sink[TALL_VISITS] = jnp.zeros((TALL, NZ), F32)

    def put(k, i, x):
        high, low = halves(x)
        rows = pl.ds(pl.multiple_of(lax.rem(i, 2) * NY, NY), NY)
        fmat[i // 2, k, rows, 0:NZ] = high
        fmat[i // 2, k, rows, NZ : 2 * NZ] = low

    def pick(fields):
        lo, hi = fields
        count = hi - lo
        found = []
        for at, window, start in visits:
            hot = oh_group[at]
            part = jnp.dot(
                fmat[window, lo:hi].reshape(count * WIDTH, 2 * NZ),
                jnp.concatenate([hot, hot], axis=0),
                preferred_element_type=F32,
            )
            wanted = jnp.where(start < 0, -1, row_group[at] - start)
            hit = row_hit(wanted, WIDTH)
            found.append(
                [
                    jnp.sum(
                        jnp.where(hit, part[f * WIDTH : (f + 1) * WIDTH], 0.0),
                        axis=0,
                        keepdims=True,
                    )
                    for f in range(count)
                ]
            )
        for k in range(GROUPS):
            for f in range(count):
                total = jnp.zeros((1, GROUP), F32)
                for (at, _, _), values in zip(visits, found):
                    total = total + jnp.where(at == k, values[f], 0.0)
                fv[lo + f, :, k * GROUP : (k + 1) * GROUP] = total

    @pl.loop(0, NX, unroll=2)
    def _(i):
        t, tw = t0p[i + 1], te[i]
        lifted = t - bath
        growth = rate(st[i]) * (1.0 - f0[i]) * gate(t)
        new = f0[i] + growth
        f1[i] = new
        tb[i] = enthalpy * growth
        slope = (enthalpy * tw + pe[i]) * (rate(st[i]) * (1.0 - new)) * -sharpness
        put(0, i, lifted)
        put(1, i, tw * lifted)
        put(2, i, slope * lifted)

    def gather(matrix, size, hot, row, out):
        found = jnp.dot(
            matrix[...], jnp.concatenate([hot, hot], axis=0), preferred_element_type=F32
        )
        found = jnp.where(row_hit(row, size), found, 0.0)
        out[...] = jnp.sum(found, axis=0, keepdims=True)

    def scatter(value, hot, left):
        high, low = halves(value)
        right = jnp.concatenate(
            [hot * jnp.broadcast_to(high, hot.shape), hot * jnp.broadcast_to(low, hot.shape)],
            axis=1,
        )
        return lax.dot_general(
            jnp.concatenate([left, left], axis=1),
            right,
            (((1,), (1,)), ((), ())),
            preferred_element_type=F32,
        )

    def row_marks(ref):
        return jnp.where(row_hit(ref[...], HROWS), 1.0, 0.0).astype(BF16)

    def hot_lanes(ref):
        return one_hot(ref[...].astype(BF16), column[...], 256)

    pick((0, 3))
    fv[0] = ext[...] * fv[0]
    fv[1] = ext[...] * (ext[...] * fv[1])
    fv[2] = ext[...] * fv[2]
    early = send(fv.at[pl.ds(0, 3)], pfv.at[pl.ds(0, 3)], 17, partner)

    def slot_gradient(value, kept):
        g = gate(kept[3] - value * kept[0])
        return 2.0 * value * kept[1] - kept[4] - kept[2] * (g * (1.0 - g))


    loads["coef"].wait()
    for copy in table:
        copy.wait_recv()
    pieces = []
    for part in range(2):
        pieces.append(halves(tab[:, part].reshape(HROWS, 128)))
    tmat[...] = jnp.concatenate(
        [pieces[0][0], pieces[1][0], pieces[0][1], pieces[1][1]], axis=1
    )

    request.wait_recv()
    row, lane = decode(ploc[...], gx, zh)
    row_b[...], lane_b[...] = row, lane.astype(F32)
    hot_b[...] = hot_lanes(lane_b)
    gather(tmat, HROWS, hot_b[...], row_b[...], val_b)
    reply = send(val_b, ret, 16, partner)

    for copy in halo:
        copy.wait_recv()
    for arrived in halo_x:
        arrived()
    outer.wait_recv()
    yr[0] = jnp.where(gy > 0, yr[0], 0.0)
    yr[1] = jnp.where(gy < 3, yr[1], 0.0)

    def z_halo(inner, outer):
        outer = jnp.where(outer_live, outer, 0.0)
        return z_block(jnp.where(even, outer, inner), jnp.where(even, inner, outer))

    for k in range(2):
        zt[k] = z_halo(zr[0, k : k + 1], zr[1, k : k + 1])

    @pl.loop(0, NX, unroll=2)
    def _(i):
        t = t0p[i + 1]
        around = neighbours(t, t0p[i], t0p[i + 2], yr[0, 0, i], yr[1, 0, i], zt[0, i])
        adjoint = neighbours(wp[i + 1], wp[i], wp[i + 2], yr[0, 1, i], yr[1, 1, i], zt[1, i])
        d, tw = dn[i], te[i]
        plain = t + d * (around - 6.0 * t) + tb[i]
        tb[i] = plain
        put(3, i, plain)
        put(4, i, tw * (plain - bath) + (tw * (1.0 - 6.0 * d) + adjoint) * (t - bath))

    pick((3, 5))
    fv[4] = ext[...] * fv[4]
    late = send(fv.at[pl.ds(3, 2)], pfv.at[pl.ds(3, 2)], 31, partner)
    hot_a[...] = hot_lanes(lane_a)
    gather(tmat, HROWS, hot_a[...], row_a[...], val_a)

    sg[...] = slot_gradient(val_a[...], fv)
    acc[...] = scatter(sg[...], hot_a[...], row_marks(row_a))
    left_b[...] = row_marks(row_b)

    reply.wait_recv()
    val_a[...] = ext[...] * (val_a[...] + ret[...])
    high, low = halves(val_a[...])
    for k in range(GROUPS):
        cols = slice(k * GROUP, (k + 1) * GROUP)
        hot = oh_group[k]
        slopes[k, :, 0:GROUP] = hot * jnp.broadcast_to(high[:, cols], hot.shape)
        slopes[k, :, GROUP : 2 * GROUP] = hot * jnp.broadcast_to(low[:, cols], hot.shape)
    running = None
    for k, (at, window, _) in enumerate(tall):
        rise = rises[k]
        part = lax.dot_general(
            jnp.concatenate([rise, rise], axis=1),
            slopes[at],
            (((1,), (1,)), ((), ())),
            preferred_element_type=F32,
        )
        if k:
            part = part + jnp.where(window == tall[k - 1][1], running, 0.0)
        sink[k] = part
        running = part

    per = TALL // NY
    for w, end in enumerate(ends):
        for k in range(per):
            i = w * per + k
            drain = sink[end, k * NY : (k + 1) * NY, :]
            t1p[i + 1] = tb[i] - drain * (t0p[i + 1] - bath)

    ys1[0] = t1p[1:17, 0:1, :]
    ys1[1] = t1p[1:17, NY - 1 : NY, :]
    left, right = z_faces(t1p[1:17])
    zs1[0] = jnp.where(even, right, left)
    zs1[1] = jnp.where(even, left, right)
    halo = [
        send(zs1.at[1], zr1.at[1], 18, partner),
        send(zs1.at[0], zr1.at[0], 19, mate),
        send(ys1.at[0], yr1.at[1], 22, y_down),
        send(ys1.at[1], yr1.at[0], 23, y_up),
    ]
    halo_x = send_x(t1p, 20)
    early.wait_recv()
    late.wait_recv()
    psg[...] = slot_gradient(val_b[...], pfv)
    acc[...] += scatter(psg[...], hot_b[...], left_b[...])
    for g in range(4):
        for part in range(2):
            spread[part, g] = acc[g * CROWS : (g + 1) * CROWS, part * 128 : (part + 1) * 128]
    swap = send(spread.at[1 - c], theirs, 24, mate)
    swap.wait_recv()
    mine[...] = spread[c] + theirs[...]
    shares = []
    for k, far in enumerate((2, 1, 3)):
        to = lax.rem(gy + far, 4)
        shares.append((send(mine.at[to], rs.at[k], 25 + k, (gx, to, gz)), k))

    for w, end in enumerate(ends):

        @pl.loop(0, per, unroll=2)
        def _(k):
            i = w * per + k
            drain = sink[end, pl.ds(pl.multiple_of(k * NY, NY), NY), :]
            t1 = t1p[i + 1]
            growth = rate(st[i]) * (1.0 - f1[i]) * gate(t1)
            f2[i] = f1[i] + growth
            t2[i] = t1 - 6.0 * dn[i] * t1 + enthalpy * growth - drain * (t1 - bath)

    for copy in halo[1:]:
        copy.wait_recv()
    halo_x()
    yr1[0] = jnp.where(gy > 0, yr1[0], 0.0)
    yr1[1] = jnp.where(gy < 3, yr1[1], 0.0)
    zt[0] = z_halo(zr1[0], jnp.zeros((1, ROWS), F32))

    @pl.loop(0, NX, unroll=4)
    def _(i):
        around = neighbours(
            t1p[i + 1], t1p[i], t1p[i + 2], yr1[0, i], yr1[1, i], zt[0, i]
        )
        t2[i] = t2[i] + dn[i] * around

    halo[0].wait_recv()
    outside = jnp.where(outer_live, zr1[1], 0.0)
    outside = z_block(jnp.where(even, outside, 0.0), jnp.where(even, 0.0, outside))
    tile = pl.ds(pl.multiple_of((1 - even.astype(I32)) * 128, 128), 128)
    t2[:, :, tile] = t2[:, :, tile] + dn[:, :, tile] * outside

    total = mine[gy]
    for copy, k in shares:
        copy.wait_recv()
        total = total + rs[k]
    sens[...] = total
    for wait in sent:
        wait()


def deliver(t2, f2, sens, temp_out, frac_out, sens_out, sem):
    copies = [
        pltpu.make_async_copy(source, target, sem.at[k])
        for k, (source, target) in enumerate(((t2, temp_out), (f2, frac_out), (sens, sens_out)))
    ]
    for copy in copies:
        copy.start()
    for copy in copies:
        copy.wait()


def on_device(t0, f0, dn, st, coef, cell, loc, ext, active, te, pe):
    field = (NX, NY, NZ)
    padded = (NX + 2, NY, NZ)
    row = (1, SLOTS)
    vmem = pltpu.VMEM
    anywhere = pl.BlockSpec(memory_space=pl.ANY)
    scratch = (
        [vmem(padded, F32)] * 3
        + [vmem(field, F32)] * 2
        + [vmem(field, I32)]
        + [vmem(field, F32)] * 4
        + [
            vmem((4, 2, CROWS, 128), F32),
            vmem((3, CROWS, 128), F32),
            vmem((2, 4, CROWS, 128), F32),
            vmem((4, CROWS, 128), F32),
            vmem((4, CROWS, 128), F32),
            pltpu.SMEM((1,), I32),
            vmem(row, I32),
            pltpu.SMEM(row, I32),
            vmem(row, I32),
            vmem(row, I32),
            vmem(row, F32),
        ]
        + [vmem(row, I32)]
        + [vmem(row, F32), vmem(row, I32)] * 2
        + [vmem(row, F32)] * 5
        + [vmem((2, 2, NX, 1, NZ), F32)] * 2
        + [vmem((2, NX, 1, NZ), F32)] * 2
        + [vmem((2, 2, ROWS), F32)] * 2
        + [vmem((2, 1, ROWS), F32)] * 2
        + [
            vmem((2, NX, NY, 128), F32),
            vmem((TALL_VISITS + 1, TALL, NZ), F32),
            vmem((HROWS, 256), F32),
            vmem((HROWS, 512), BF16),
            vmem((WINDOWS, 5, WIDTH, 512), BF16),
            vmem((5, 1, SLOTS), F32),
            vmem((5, 1, SLOTS), F32),
            vmem((256, SLOTS), BF16),
            vmem((256, SLOTS), BF16),
            vmem((HROWS, SLOTS), BF16),
            vmem((TALL_VISITS, TALL, GROUP), BF16),
            vmem((GROUPS, NZ, 2 * GROUP), BF16),
            vmem((NZ, SLOTS), BF16),
            vmem((GROUPS, NZ, GROUP), BF16),
            vmem((GROUPS, 1, GROUP), I32),
            vmem((256, 128), BF16),
            pltpu.SemaphoreType.DMA((12,)),
            pltpu.SemaphoreType.DMA((32,)),
            pltpu.SemaphoreType.DMA((32,)),
        ]
    )
    results = (
        jax.ShapeDtypeStruct(field, F32),
        jax.ShapeDtypeStruct(field, F32),
        jax.ShapeDtypeStruct((CROWS, 128), F32),
    )
    done = pl.pallas_call(
        kernel,
        out_shape=(vmem(field, F32), vmem(field, F32), vmem((CROWS, 128), F32)),
        in_specs=[anywhere] * 11,
        out_specs=(pl.BlockSpec(memory_space=vmem),) * 3,
        scratch_shapes=scratch,
        compiler_params=pltpu.CompilerParams(
            collective_id=0, has_side_effects=True, vmem_limit_bytes=56 * 2**20
        ),
    )(
        active,
        t0,
        f0,
        dn,
        st,
        coef.reshape(CROWS, 128),
        cell.reshape(row),
        loc.reshape(row),
        ext.reshape(row),
        te,
        pe,
    )
    temp, frac, sens = pl.pallas_call(
        deliver,
        out_shape=results,
        in_specs=[anywhere] * 3,
        out_specs=(anywhere,) * 3,
        scratch_shapes=[pltpu.SemaphoreType.DMA((3,))],
        compiler_params=pltpu.CompilerParams(vmem_limit_bytes=2**20),
    )(*done)
    return temp, frac, sens.reshape(CHUNK)


def solution(mesh):
    brick, line = P("gx", "gy", "gz"), P(("gx", "gy", "gz"))
    return jax.shard_map(
        on_device,
        mesh=mesh,
        in_specs=(brick,) * 4 + (line,) * 5 + (brick,) * 2,
        out_specs=(brick, brick, line),
        check_vma=False,
    )
```

```python
import functools

import jax
import jax.numpy as jnp
from jax import lax
from jax.experimental import pallas as pl
from jax.experimental.pallas import tpu as pltpu
from jax.sharding import PartitionSpec as P

MESH = pl.DeviceIdType.MESH
F32 = jnp.float32
BF16 = jnp.bfloat16
I32 = jnp.int32

NX, NY, NZ = 16, 32, 256
ROWS = NX * NY
SLOTS = 2048
CHUNK = 7168
CROWS = CHUNK // 128
HROWS = 4 * CROWS
SLAB = 16 * CHUNK
GROUP = 256
GROUPS = SLOTS // GROUP
WIDTH = 64
WINDOWS = ROWS // WIDTH
VISITS = GROUPS + WINDOWS - 1
TALL = 128
TALL_WINDOWS = ROWS // TALL
TALL_VISITS = GROUPS + TALL_WINDOWS - 1

sharpness = 4.0
kinetic_fast = 0.6
kinetic_slow = 0.2
enthalpy = 0.4
bath = -2.0


def halves(x):
    high = x.astype(BF16)
    return high, (x - high.astype(F32)).astype(BF16)


def one_hot(index, column, size):
    column = jnp.concatenate([column] * (index.shape[1] // 128), axis=1)
    hit = column == jnp.broadcast_to(index, (size, index.shape[1]))
    return jnp.where(hit, jnp.ones((), BF16), jnp.zeros((), BF16))


def row_hit(index, size):
    rows = lax.broadcasted_iota(I32, (size, index.shape[1]), 0)
    return rows == index


def gate(t):
    return jax.nn.sigmoid(sharpness * (0.0 - t))


def rate(status):
    return jnp.where(status == 1, kinetic_fast, jnp.where(status == 2, kinetic_slow, 0.0))


def decode(loc, gx, zh):
    local = loc - gx * SLAB
    row = local >> 7
    owner = (row * 1171) >> 16
    inner = row - owner * CROWS
    mine = ((owner >> 1) & 1) == zh
    return jnp.where(mine, (owner >> 2) * CROWS + inner, -1), (owner & 1) * 128 + (local & 127)


def neighbours(center, low, high, y_low, y_high, z_edge):
    y = lax.broadcasted_iota(I32, (NY, NZ), 0)
    z = lax.broadcasted_iota(I32, (NY, NZ), 1)
    edge = jnp.concatenate([z_edge, z_edge], axis=1)
    total = low + high
    total = total + jnp.where(y == 0, y_low, pltpu.roll(center, 1, 0))
    total = total + jnp.where(y == NY - 1, y_high, pltpu.roll(center, NY - 1, 0))
    total = total + jnp.where(z == 0, edge, pltpu.roll(center, 1, 1))
    return total + jnp.where(z == NZ - 1, edge, pltpu.roll(center, NZ - 1, 1))


def z_faces(x):
    x = x.reshape(ROWS, NZ)
    lane = lax.broadcasted_iota(I32, (ROWS, 128), 1)
    both = jnp.where(lane == 0, x[:, :128], x[:, 128:]).T
    return both[0:1, :], both[127:128, :]


def z_block(left, right):
    row = lax.broadcasted_iota(I32, (128, ROWS), 0)
    both = jnp.where(row == 0, left, jnp.where(row == 127, right, 0.0))
    return both.T.reshape(NX, NY, 128)


def kernel(
    live_hbm,
    t0_hbm,
    f0_hbm,
    dn_hbm,
    st_hbm,
    coef_hbm,
    cell_hbm,
    loc_hbm,
    ext_hbm,
    te_hbm,
    pe_hbm,
    t2,
    f2,
    sens,
    t0p,
    wp,
    t1p,
    f0,
    dn,
    st,
    te,
    pe,
    tb,
    f1,
    tab,
    rs,
    spread,
    theirs,
    mine,
    active,
    cell,
    mark,
    loc,
    ploc,
    ext,
    row_c,
    lane_a,
    row_a,
    lane_b,
    row_b,
    val_a,
    val_b,
    ret,
    sg,
    psg,
    ys,
    yr,
    ys1,
    yr1,
    zs,
    zr,
    zs1,
    zr1,
    zt,
    sink,
    acc,
    tmat,
    fmat,
    fv,
    pfv,
    hot_a,
    hot_b,
    left_b,
    rises,
    slopes,
    oh_lane,
    oh_group,
    row_group,
    column,
    load_sem,
    send_sem,
    recv_sem,
):
    gx, gy, gz = lax.axis_index("gx"), lax.axis_index("gy"), lax.axis_index("gz")
    zh, c = gz // 2, gz % 2
    even = c == 0
    outer_live = jnp.logical_or(gz == 1, gz == 2)
    partner = (gx, gy, 3 - gz)
    mate = (gx, gy, zh * 2 + (1 - c))
    x_up, x_down = (jnp.minimum(gx + 1, 15), gy, gz), (jnp.maximum(gx - 1, 0), gy, gz)
    has_up, has_down = gx < 15, gx > 0
    y_up, y_down = (gx, lax.rem(gy + 1, 4), gz), (gx, lax.rem(gy + 3, 4), gz)
    peers = []
    for j in (4, 5, 2, 3, 6, 7, 1):
        pgy, pc = lax.rem(gy + j // 2, 4), lax.rem(c + j % 2, 2)
        peers.append((j, pgy, pc, (gx, pgy, zh * 2 + pc)))

    barrier = pltpu.get_barrier_semaphore()

    def greet(device):
        pl.semaphore_signal(barrier, inc=1, device_id=device, device_id_type=MESH)

    greet(partner)
    pl.when(has_up)(lambda: greet(x_up))
    pl.when(has_down)(lambda: greet(x_down))
    for _, _, _, device in peers:
        greet(device)
    expected = 7 + has_up.astype(I32) + has_down.astype(I32) + 1

    loads = {}
    for k, (name, source, target) in enumerate(
        (
            ("t0", t0_hbm, t0p.at[pl.ds(1, NX)]),
            ("dn", dn_hbm, dn),
            ("te", te_hbm, te),
            ("cell", cell_hbm, cell),
            ("mark", cell_hbm, mark),
            ("active", live_hbm, active),
            ("loc", loc_hbm, loc),
            ("ext", ext_hbm, ext),
            ("coef", coef_hbm, tab.at[gy, c]),
            ("f0", f0_hbm, f0),
            ("st", st_hbm, st),
            ("pe", pe_hbm, pe),
        )
    ):
        loads[name] = pltpu.make_async_copy(source, target, load_sem.at[k])
        loads[name].start()

    sent = []

    def remote(source, target, index, device):
        return pltpu.make_async_remote_copy(
            src_ref=source,
            dst_ref=target,
            send_sem=send_sem.at[index],
            recv_sem=recv_sem.at[index],
            device_id=device,
            device_id_type=MESH,
        )

    def send(source, target, index, device):
        copy = remote(source, target, index, device)
        copy.start()
        sent.append(copy.wait_send)
        return copy

    def send_x(padded, index):
        down = remote(padded.at[1], padded.at[NX + 1], index, x_down)
        up = remote(padded.at[NX], padded.at[0], index + 1, x_up)
        pl.when(has_down)(down.start)
        pl.when(has_up)(up.start)
        sent.append(lambda: pl.when(has_down)(down.wait_send))
        sent.append(lambda: pl.when(has_up)(up.wait_send))

        def arrived():
            pl.when(has_up)(down.wait_recv)
            pl.when(has_down)(up.wait_recv)
            padded[0] = jnp.where(has_down, padded[0], 0.0)
            padded[NX + 1] = jnp.where(has_up, padded[NX + 1], 0.0)

        return arrived

    base = lax.broadcasted_iota(I32, (256, 128), 0).astype(F32).astype(BF16)
    column[...] = base

    loads["t0"].wait()
    loads["dn"].wait()
    loads["te"].wait()

    @pl.loop(0, NX, unroll=2)
    def _(i):
        wp[i + 1] = dn[i] * te[i]

    for k, padded in enumerate((t0p, wp)):
        ys[0, k] = padded[1:17, 0:1, :]
        ys[1, k] = padded[1:17, NY - 1 : NY, :]
        left, right = z_faces(padded[1:17])
        zs[0, k : k + 1] = jnp.where(even, right, left)
        zs[1, k : k + 1] = jnp.where(even, left, right)

    pl.semaphore_wait(barrier, expected)
    request = send(loc_hbm, ploc, 0, partner)
    outer = send(zs.at[1], zr.at[1], 8, partner)
    table = {
        j: send(coef_hbm, tab.at[gy, c], j, device)
        for j, _, _, device in peers
        if j % 2 == 0 or j == 1
    }
    halo = [
        send(zs.at[0], zr.at[0], 9, mate),
        send(ys.at[0], yr.at[1], 14, y_down),
        send(ys.at[1], yr.at[0], 15, y_up),
    ]
    halo_x = [send_x(t0p, 10), send_x(wp, 12)]

    for name in ("cell", "loc", "ext"):
        loads[name].wait()
    loads["mark"].wait()
    loads["active"].wait()
    cell_row = cell[...] >> 8
    oh_lane[...] = one_hot((cell[...] & (NZ - 1)).astype(F32).astype(BF16), column[...], NZ)
    row_c[...] = cell_row
    row, lane = decode(loc[...], gx, zh)
    row_a[...], lane_a[...] = row, lane.astype(F32)
    slot = lax.broadcasted_iota(I32, (1, SLOTS), 1)
    ext[...] = jnp.where(slot < active[0], ext[...], 0.0)
    for name in ("f0", "st", "pe"):
        loads[name].wait()

    def path(count, width):
        visits = []
        group, window = jnp.int32(0), jnp.int32(0)
        for _ in range(count):
            over = group >= GROUPS
            at = jnp.minimum(group, GROUPS - 1)
            visits.append((at, window, jnp.where(over, -1, window * width)))
            last = mark[0, at * GROUP + (GROUP - 1)] >> 8
            more = jnp.logical_and(last >= (window + 1) * width, jnp.logical_not(over))
            window = jnp.where(more, window + 1, window)
            group = jnp.where(more, group, group + 1)
        return visits

    visits, tall = path(VISITS, WIDTH), path(TALL_VISITS, TALL)

    for k in range(GROUPS):
        oh_group[k] = oh_lane[:, k * GROUP : (k + 1) * GROUP]
        row_group[k] = row_c[:, k * GROUP : (k + 1) * GROUP]

    ends = [jnp.int32(TALL_VISITS)] * TALL_WINDOWS
    for k, (at, window, start) in enumerate(tall):
        wanted = jnp.where(start < 0, -1, row_group[at] - start)
        rises[k] = jnp.where(row_hit(wanted, TALL), 1.0, 0.0).astype(BF16)
        ends = [jnp.where(window == w, k, end) for w, end in enumerate(ends)]
    sink[TALL_VISITS] = jnp.zeros((TALL, NZ), F32)

    def put(k, i, x):
        high, low = halves(x)
        rows = pl.ds(pl.multiple_of(lax.rem(i, 2) * NY, NY), NY)
        fmat[i // 2, k, rows, 0:NZ] = high
        fmat[i // 2, k, rows, NZ : 2 * NZ] = low

    def pick(fields):
        lo, hi = fields
        count = hi - lo
        found = []
        for at, window, start in visits:
            hot = oh_group[at]
            part = jnp.dot(
                fmat[window, lo:hi].reshape(count * WIDTH, 2 * NZ),
                jnp.concatenate([hot, hot], axis=0),
                preferred_element_type=F32,
            )
            wanted = jnp.where(start < 0, -1, row_group[at] - start)
            hit = row_hit(wanted, WIDTH)
            found.append(
                [
                    jnp.sum(
                        jnp.where(hit, part[f * WIDTH : (f + 1) * WIDTH], 0.0),
                        axis=0,
                        keepdims=True,
                    )
                    for f in range(count)
                ]
            )
        for k in range(GROUPS):
            for f in range(count):
                total = jnp.zeros((1, GROUP), F32)
                for (at, _, _), values in zip(visits, found):
                    total = total + jnp.where(at == k, values[f], 0.0)
                fv[lo + f, :, k * GROUP : (k + 1) * GROUP] = total

    @pl.loop(0, NX, unroll=2)
    def _(i):
        t, tw = t0p[i + 1], te[i]
        lifted = t - bath
        growth = rate(st[i]) * (1.0 - f0[i]) * gate(t)
        new = f0[i] + growth
        f1[i] = new
        tb[i] = enthalpy * growth
        slope = (enthalpy * tw + pe[i]) * (rate(st[i]) * (1.0 - new)) * -sharpness
        put(0, i, lifted)
        put(1, i, tw * lifted)
        put(2, i, slope * lifted)

    def gather(matrix, size, hot, row, out):
        found = jnp.dot(
            matrix[...], jnp.concatenate([hot, hot], axis=0), preferred_element_type=F32
        )
        found = jnp.where(row_hit(row, size), found, 0.0)
        out[...] = jnp.sum(found, axis=0, keepdims=True)

    def scatter(value, hot, left):
        high, low = halves(value)
        right = jnp.concatenate(
            [hot * jnp.broadcast_to(high, hot.shape), hot * jnp.broadcast_to(low, hot.shape)],
            axis=1,
        )
        return lax.dot_general(
            jnp.concatenate([left, left], axis=1),
            right,
            (((1,), (1,)), ((), ())),
            preferred_element_type=F32,
        )

    def row_marks(ref):
        return jnp.where(row_hit(ref[...], HROWS), 1.0, 0.0).astype(BF16)

    def hot_lanes(ref):
        return one_hot(ref[...].astype(BF16), column[...], 256)

    pick((0, 3))
    fv[0] = ext[...] * fv[0]
    fv[1] = ext[...] * (ext[...] * fv[1])
    fv[2] = ext[...] * fv[2]
    early = send(fv.at[pl.ds(0, 3)], pfv.at[pl.ds(0, 3)], 17, partner)

    def slot_gradient(value, kept):
        g = gate(kept[3] - value * kept[0])
        return 2.0 * value * kept[1] - kept[4] - kept[2] * (g * (1.0 - g))


    loads["coef"].wait()
    passed = [table[1]]
    for j in (2, 6, 4):
        table[j].wait_recv()
        chunk = tab.at[lax.rem(gy + 4 - j // 2, 4), c]
        passed.append(send(chunk, chunk, j + 1, mate))
    for copy in passed:
        copy.wait_recv()
    pieces = []
    for part in range(2):
        pieces.append(halves(tab[:, part].reshape(HROWS, 128)))
    tmat[...] = jnp.concatenate(
        [pieces[0][0], pieces[1][0], pieces[0][1], pieces[1][1]], axis=1
    )

    request.wait_recv()
    row, lane = decode(ploc[...], gx, zh)
    row_b[...], lane_b[...] = row, lane.astype(F32)
    hot_b[...] = hot_lanes(lane_b)
    gather(tmat, HROWS, hot_b[...], row_b[...], val_b)
    reply = send(val_b, ret, 16, partner)

    for copy in halo:
        copy.wait_recv()
    for arrived in halo_x:
        arrived()
    outer.wait_recv()
    yr[0] = jnp.where(gy > 0, yr[0], 0.0)
    yr[1] = jnp.where(gy < 3, yr[1], 0.0)

    def z_halo(inner, outer):
        outer = jnp.where(outer_live, outer, 0.0)
        return z_block(jnp.where(even, outer, inner), jnp.where(even, inner, outer))

    for k in range(2):
        zt[k] = z_halo(zr[0, k : k + 1], zr[1, k : k + 1])

    @pl.loop(0, NX, unroll=2)
    def _(i):
        t = t0p[i + 1]
        around = neighbours(t, t0p[i], t0p[i + 2], yr[0, 0, i], yr[1, 0, i], zt[0, i])
        adjoint = neighbours(wp[i + 1], wp[i], wp[i + 2], yr[0, 1, i], yr[1, 1, i], zt[1, i])
        d, tw = dn[i], te[i]
        plain = t + d * (around - 6.0 * t) + tb[i]
        tb[i] = plain
        put(3, i, plain)
        put(4, i, tw * (plain - bath) + (tw * (1.0 - 6.0 * d) + adjoint) * (t - bath))

    pick((3, 5))
    fv[4] = ext[...] * fv[4]
    late = send(fv.at[pl.ds(3, 2)], pfv.at[pl.ds(3, 2)], 31, partner)
    hot_a[...] = hot_lanes(lane_a)
    gather(tmat, HROWS, hot_a[...], row_a[...], val_a)

    sg[...] = slot_gradient(val_a[...], fv)
    acc[...] = scatter(sg[...], hot_a[...], row_marks(row_a))
    left_b[...] = row_marks(row_b)

    reply.wait_recv()
    val_a[...] = ext[...] * (val_a[...] + ret[...])
    high, low = halves(val_a[...])
    for k in range(GROUPS):
        cols = slice(k * GROUP, (k + 1) * GROUP)
        hot = oh_group[k]
        slopes[k, :, 0:GROUP] = hot * jnp.broadcast_to(high[:, cols], hot.shape)
        slopes[k, :, GROUP : 2 * GROUP] = hot * jnp.broadcast_to(low[:, cols], hot.shape)
    running = None
    for k, (at, window, _) in enumerate(tall):
        rise = rises[k]
        part = lax.dot_general(
            jnp.concatenate([rise, rise], axis=1),
            slopes[at],
            (((1,), (1,)), ((), ())),
            preferred_element_type=F32,
        )
        if k:
            part = part + jnp.where(window == tall[k - 1][1], running, 0.0)
        sink[k] = part
        running = part

    per = TALL // NY
    for w, end in enumerate(ends):
        for k in range(per):
            i = w * per + k
            drain = sink[end, k * NY : (k + 1) * NY, :]
            t1p[i + 1] = tb[i] - drain * (t0p[i + 1] - bath)

    ys1[0] = t1p[1:17, 0:1, :]
    ys1[1] = t1p[1:17, NY - 1 : NY, :]
    left, right = z_faces(t1p[1:17])
    zs1[0] = jnp.where(even, right, left)
    zs1[1] = jnp.where(even, left, right)
    halo = [
        send(zs1.at[1], zr1.at[1], 18, partner),
        send(zs1.at[0], zr1.at[0], 19, mate),
        send(ys1.at[0], yr1.at[1], 22, y_down),
        send(ys1.at[1], yr1.at[0], 23, y_up),
    ]
    halo_x = send_x(t1p, 20)
    early.wait_recv()
    late.wait_recv()
    psg[...] = slot_gradient(val_b[...], pfv)
    acc[...] += scatter(psg[...], hot_b[...], left_b[...])
    for g in range(4):
        for part in range(2):
            spread[part, g] = acc[g * CROWS : (g + 1) * CROWS, part * 128 : (part + 1) * 128]
    swap = send(spread.at[1 - c], theirs, 24, mate)
    swap.wait_recv()
    mine[...] = spread[c] + theirs[...]
    shares = []
    for k, far in enumerate((2, 1, 3)):
        to = lax.rem(gy + far, 4)
        shares.append((send(mine.at[to], rs.at[k], 25 + k, (gx, to, gz)), k))

    for w, end in enumerate(ends):

        @pl.loop(0, per, unroll=2)
        def _(k):
            i = w * per + k
            drain = sink[end, pl.ds(pl.multiple_of(k * NY, NY), NY), :]
            t1 = t1p[i + 1]
            growth = rate(st[i]) * (1.0 - f1[i]) * gate(t1)
            f2[i] = f1[i] + growth
            t2[i] = t1 - 6.0 * dn[i] * t1 + enthalpy * growth - drain * (t1 - bath)

    for copy in halo[1:]:
        copy.wait_recv()
    halo_x()
    yr1[0] = jnp.where(gy > 0, yr1[0], 0.0)
    yr1[1] = jnp.where(gy < 3, yr1[1], 0.0)
    zt[0] = z_halo(zr1[0], jnp.zeros((1, ROWS), F32))

    @pl.loop(0, NX, unroll=4)
    def _(i):
        around = neighbours(
            t1p[i + 1], t1p[i], t1p[i + 2], yr1[0, i], yr1[1, i], zt[0, i]
        )
        t2[i] = t2[i] + dn[i] * around

    halo[0].wait_recv()
    outside = jnp.where(outer_live, zr1[1], 0.0)
    outside = z_block(jnp.where(even, outside, 0.0), jnp.where(even, 0.0, outside))
    tile = pl.ds(pl.multiple_of((1 - even.astype(I32)) * 128, 128), 128)
    t2[:, :, tile] = t2[:, :, tile] + dn[:, :, tile] * outside

    total = mine[gy]
    for copy, k in shares:
        copy.wait_recv()
        total = total + rs[k]
    sens[...] = total
    for wait in sent:
        wait()


def deliver(t2, f2, sens, temp_out, frac_out, sens_out, sem):
    copies = [
        pltpu.make_async_copy(source, target, sem.at[k])
        for k, (source, target) in enumerate(((t2, temp_out), (f2, frac_out), (sens, sens_out)))
    ]
    for copy in copies:
        copy.start()
    for copy in copies:
        copy.wait()


def on_device(t0, f0, dn, st, coef, cell, loc, ext, active, te, pe):
    field = (NX, NY, NZ)
    padded = (NX + 2, NY, NZ)
    row = (1, SLOTS)
    vmem = pltpu.VMEM
    anywhere = pl.BlockSpec(memory_space=pl.ANY)
    scratch = (
        [vmem(padded, F32)] * 3
        + [vmem(field, F32)] * 2
        + [vmem(field, I32)]
        + [vmem(field, F32)] * 4
        + [
            vmem((4, 2, CROWS, 128), F32),
            vmem((3, CROWS, 128), F32),
            vmem((2, 4, CROWS, 128), F32),
            vmem((4, CROWS, 128), F32),
            vmem((4, CROWS, 128), F32),
            pltpu.SMEM((1,), I32),
            vmem(row, I32),
            pltpu.SMEM(row, I32),
            vmem(row, I32),
            vmem(row, I32),
            vmem(row, F32),
        ]
        + [vmem(row, I32)]
        + [vmem(row, F32), vmem(row, I32)] * 2
        + [vmem(row, F32)] * 5
        + [vmem((2, 2, NX, 1, NZ), F32)] * 2
        + [vmem((2, NX, 1, NZ), F32)] * 2
        + [vmem((2, 2, ROWS), F32)] * 2
        + [vmem((2, 1, ROWS), F32)] * 2
        + [
            vmem((2, NX, NY, 128), F32),
            vmem((TALL_VISITS + 1, TALL, NZ), F32),
            vmem((HROWS, 256), F32),
            vmem((HROWS, 512), BF16),
            vmem((WINDOWS, 5, WIDTH, 512), BF16),
            vmem((5, 1, SLOTS), F32),
            vmem((5, 1, SLOTS), F32),
            vmem((256, SLOTS), BF16),
            vmem((256, SLOTS), BF16),
            vmem((HROWS, SLOTS), BF16),
            vmem((TALL_VISITS, TALL, GROUP), BF16),
            vmem((GROUPS, NZ, 2 * GROUP), BF16),
            vmem((NZ, SLOTS), BF16),
            vmem((GROUPS, NZ, GROUP), BF16),
            vmem((GROUPS, 1, GROUP), I32),
            vmem((256, 128), BF16),
            pltpu.SemaphoreType.DMA((12,)),
            pltpu.SemaphoreType.DMA((32,)),
            pltpu.SemaphoreType.DMA((32,)),
        ]
    )
    results = (
        jax.ShapeDtypeStruct(field, F32),
        jax.ShapeDtypeStruct(field, F32),
        jax.ShapeDtypeStruct((CROWS, 128), F32),
    )
    done = pl.pallas_call(
        kernel,
        out_shape=(vmem(field, F32), vmem(field, F32), vmem((CROWS, 128), F32)),
        in_specs=[anywhere] * 11,
        out_specs=(pl.BlockSpec(memory_space=vmem),) * 3,
        scratch_shapes=scratch,
        compiler_params=pltpu.CompilerParams(
            collective_id=0, has_side_effects=True, vmem_limit_bytes=56 * 2**20
        ),
    )(
        active,
        t0,
        f0,
        dn,
        st,
        coef.reshape(CROWS, 128),
        cell.reshape(row),
        loc.reshape(row),
        ext.reshape(row),
        te,
        pe,
    )
    temp, frac, sens = pl.pallas_call(
        deliver,
        out_shape=results,
        in_specs=[anywhere] * 3,
        out_specs=(anywhere,) * 3,
        scratch_shapes=[pltpu.SemaphoreType.DMA((3,))],
        compiler_params=pltpu.CompilerParams(vmem_limit_bytes=2**20),
    )(*done)
    return temp, frac, sens.reshape(CHUNK)


def solution(mesh):
    brick, line = P("gx", "gy", "gz"), P(("gx", "gy", "gz"))
    return jax.shard_map(
        on_device,
        mesh=mesh,
        in_specs=(brick,) * 4 + (line,) * 5 + (brick,) * 2,
        out_specs=(brick, brick, line),
        check_vma=False,
    )
```
